256 devices in a mesh: tile: 128 (over z, x, y), sub: 2 (over core).
Axes of the slice: x: 4, y: 4, z: 8, core: 2. Of those that a mesh axis runs over, the one named last changes fastest.
Arguments:
- grid: bfloat16 [262144, 512], P(('tile', 'sub')), may hold values from -6 to 6
- g2m_owner: int32 [2048], P(('tile', 'sub')), may hold values from 0 to 255, as said below
- g2m_weight: float32 [262144], P(('tile', 'sub')), may hold values from 0.1 to 1
- m2g_owner: int32 [2048], P(('tile', 'sub')), may hold values from 0 to 255, as said below
- m2g_weight: float32 [262144], P(('tile', 'sub')), may hold values from 0.2 to 2
- mesh_feat: bfloat16 [32768, 512], P(('tile', 'sub')), may hold values from -6 to 6
- neighbours: int32 [256, 3], P(('tile', 'sub')), may hold values from 0 to 255, as said below
- enc_w1: bfloat16 [512, 2048], replicated, may hold values from -0.25 to 0.25
- enc_w2: bfloat16 [2048, 512], replicated, may hold values from -0.125 to 0.125
- attn_gain: float32 [1, 512], replicated, may hold values from 0.25 to 1.75
- w_qkv: bfloat16 [1, 512, 1536], replicated, may hold values from -1 to 1
- w_out: bfloat16 [1, 512, 512], replicated, may hold values from -0.25 to 0.25
- dec_w1: bfloat16 [512, 2048], replicated, may hold values from -0.25 to 0.25
- dec_w2: bfloat16 [2048, 512], replicated, may hold values from -0.125 to 0.125
Outputs:
- decoded: bfloat16 [262144, 512], P(('tile', 'sub'))
- mesh_out: bfloat16 [32768, 512], P(('tile', 'sub'))
The draws below stay inside these ranges and needn't reach their ends.
Inputs may be any that keep to these rules, and one draw needn't show every extreme that they name: g2m_owner[b] equals b // 8 + e modulo 256 with e between -2 and 2; both -2 and 2 occur. m2g_owner[b] equals b // 8 + e modulo 256 with e between -2 and 2; both -2 and 2 occur. `neighbours`: row m holds three distinct blocks among m - 2, m - 1, m + 1, m + 2 modulo 256.
All inputs are finite; a program needn't handle non-finite values.
Results may differ from the reference program's by a relative error of at most 0.015.
Values may be sent and summed in bfloat16 or wider, within the bound.
A program may use at most 64 MiB of HBM per device.

```python
import math
import jax
import jax.numpy as jnp
from jax import lax

D = 512
FF = 2048
H = 4
HD = 128
BLK = 128
LAYERS = 1
GB = 8
MB = 256
GRID_BLOCKS = 2048
GRID = 262144
MESH = 32768


def owner_common(key, salt):
    offset = jax.random.randint(jax.random.fold_in(key, salt), (GRID_BLOCKS,), -2, 3)
    offset = offset.at[0].set(2).at[1].set(-2)
    base = jnp.arange(GRID_BLOCKS, dtype=jnp.int32) // GB
    return ((base + offset) % MB).astype(jnp.int32)


def draw_g2m_owner(key, part):
    return owner_common(key, 11)


def draw_m2g_owner(key, part):
    return owner_common(key, 23)


def draw_neighbours(key, part):
    keyset = jax.random.split(jax.random.fold_in(key, 5), MB)
    orders = jax.vmap(lambda single: jax.random.permutation(single, 4))(keyset)[:, :3]
    choices_table = jnp.array([-2, -1, 1, 2], dtype=jnp.int32)
    offsets = choices_table[orders]
    base = jnp.arange(MB, dtype=jnp.int32)[:, None]
    return ((base + offsets) % MB).astype(jnp.int32)


def draw_mesh_feat(key, part):
    base_key = jax.random.fold_in(key, 31)
    result = jnp.clip(jax.random.normal(base_key, (MESH, D), jnp.float32), -6.0, 6.0)
    return result.astype(jnp.bfloat16)


def draw_w_qkv(key, part):
    base_key = jax.random.fold_in(key, 41)
    scale = jnp.float32(D) ** (-0.5)
    result = jnp.clip(jax.random.normal(base_key, (LAYERS, D, 3 * D), jnp.float32), -6.0, 6.0) * scale
    return result.astype(jnp.bfloat16)


def steps_of(stream_key, shape, shards, smallest, largest):
    level = 1.0
    for position, parts in shards:
        steps = jax.random.uniform(jax.random.fold_in(jax.random.fold_in(stream_key, 6), position), (parts,), jnp.float32, smallest / len(shards), largest / len(shards))
        level = level * jnp.repeat(jnp.exp(steps), shape[position] // parts).reshape((-1,) + (1,) * (len(shape) - 1 - position))
    return level


def centred(key, shape, width, most, pieces=(), kind=jnp.bfloat16):
    values = jax.random.normal(key, shape, jnp.float32) * width
    if len(pieces) > 0:
        values = steps_of(key, shape, pieces, -0.22, 0.18) * values
    return jnp.clip(values, min=-most, max=most).astype(kind)


def setup_inputs(seed: int = 0) -> dict:
    key_list = jax.random.split(jax.random.key(seed), 15)
    grid = centred(key_list[0], (GRID, D), 1.0, 6.0, ((0, 256),))
    g2m_owner = draw_g2m_owner(jax.random.fold_in(key_list[14], 71), 0)
    g2m_weight = jnp.clip(jnp.exp(math.log(1.0) - 2.3025851 * jax.random.uniform(key_list[2], (GRID,), jnp.float32) ** steps_of(key_list[2], (GRID,), ((0, 256),), -0.2, 0.2)), 0.1, 1.0)
    m2g_owner = draw_m2g_owner(jax.random.fold_in(key_list[14], 71), 0)
    m2g_weight = jnp.clip(jnp.exp(math.log(2.0) - 2.3025851 * jax.random.uniform(key_list[4], (GRID,), jnp.float32) ** steps_of(key_list[4], (GRID,), ((0, 256),), -0.2, 0.2)), 0.2, 2.0)
    mesh_feat = draw_mesh_feat(jax.random.fold_in(key_list[14], 71), 0)
    neighbours = draw_neighbours(jax.random.fold_in(key_list[14], 71), 0)
    enc_w1 = centred(key_list[7], (D, FF), D ** -0.5, 0.25)
    enc_w2 = centred(key_list[8], (FF, D), FF ** -0.5, 0.125)
    attn_gain = jnp.clip(1.0 + 0.15 * jax.random.normal(key_list[9], (LAYERS, D), jnp.float32), 0.25, 1.75)
    w_qkv = draw_w_qkv(jax.random.fold_in(key_list[14], 71), 0)
    w_out = centred(key_list[11], (LAYERS, D, D), D ** -0.5, 0.25)
    dec_w1 = centred(key_list[12], (D, FF), D ** -0.5, 0.25)
    dec_w2 = centred(key_list[13], (FF, D), FF ** -0.5, 0.125)
    return dict(grid=grid, g2m_owner=g2m_owner, g2m_weight=g2m_weight, m2g_owner=m2g_owner, m2g_weight=m2g_weight, mesh_feat=mesh_feat, neighbours=neighbours, enc_w1=enc_w1, enc_w2=enc_w2, attn_gain=attn_gain, w_qkv=w_qkv, w_out=w_out, dec_w1=dec_w1, dec_w2=dec_w2)


def feed(rows, first, second):
    hidden = jnp.dot(rows, first, preferred_element_type=jnp.float32)
    active = jax.nn.silu(hidden).astype(jnp.bfloat16)
    return (rows.astype(jnp.float32) + jnp.dot(active, second, preferred_element_type=jnp.float32)).astype(jnp.bfloat16)

def mlp_blocks(rows, first, second):
    grouped = rows.reshape(MB, GB * BLK, D)
    result = lax.map(lambda piece: feed(piece, first, second), grouped)
    return result.reshape(GRID, D)

def reference(grid, g2m_owner, g2m_weight, m2g_owner, m2g_weight, mesh_feat, neighbours, enc_w1, enc_w2, attn_gain, w_qkv, w_out, dec_w1, dec_w2):
    encoded = mlp_blocks(grid, enc_w1, enc_w2)
    contrib = (g2m_weight[:, None] * encoded.astype(jnp.float32)).reshape(GRID_BLOCKS, BLK, D)
    added = jax.ops.segment_sum(contrib, g2m_owner, num_segments=MB)
    state = mesh_feat.astype(jnp.float32).reshape(MB, BLK, D) + added
    for layer in range(LAYERS):
        mean_sq = lax.optimization_barrier(jnp.mean(state * state, axis=-1, keepdims=True))
        normed = (state * lax.rsqrt(mean_sq + 1e-06) * attn_gain[layer]).astype(jnp.bfloat16)
        qkv = jnp.dot(normed.reshape(MESH, D), w_qkv[layer], preferred_element_type=jnp.float32).astype(jnp.bfloat16)
        qkv = qkv.reshape(MB, BLK, 3 * D)
        query = qkv[:, :, :D]
        keys = qkv[:, :, D:2 * D]
        values = qkv[:, :, 2 * D:]

        def attend(block):
            listed = jnp.concatenate([block[None], neighbours[block]]).astype(jnp.int32)
            kk = keys[listed].reshape(4 * BLK, H, HD).astype(jnp.float32)
            vv = values[listed].reshape(4 * BLK, H, HD).astype(jnp.float32)
            qq = query[block].reshape(BLK, H, HD).astype(jnp.float32)
            scores = jnp.einsum('qhd,khd->hqk', qq, kk) / jnp.sqrt(jnp.float32(HD))
            probs = jax.nn.softmax(scores, axis=-1).astype(jnp.bfloat16)
            mixed = jnp.einsum('hqk,khd->qhd', probs.astype(jnp.float32), vv)
            return mixed.astype(jnp.bfloat16).reshape(BLK, D)
        attended = lax.map(attend, jnp.arange(MB, dtype=jnp.int32))
        state = state + jnp.dot(attended.reshape(MESH, D), w_out[layer], preferred_element_type=jnp.float32).reshape(MB, BLK, D)
    mesh_out = state.astype(jnp.bfloat16)
    picked = mesh_out[m2g_owner].reshape(GRID, D)
    dec_in = (encoded.astype(jnp.float32) + m2g_weight[:, None] * picked.astype(jnp.float32)).astype(jnp.bfloat16)
    decoded = mlp_blocks(dec_in, dec_w1, dec_w2)
    return (decoded, mesh_out.reshape(MESH, D))
```

```python
import functools

import jax
import jax.numpy as jnp
from jax import lax
from jax.experimental import pallas as pl
from jax.experimental.pallas import tpu as pltpu
from jax.sharding import PartitionSpec as P

HD = 128
DELTAS = (-2, 2, -1, 1)
NEG = -1e30
BF = jnp.bfloat16
F32 = jnp.float32
NT = (((1,), (1,)), ((), ()))


def dot(a, b):
    return jnp.dot(a, b, preferred_element_type=F32)


def hidden_layer(rows, w1, hid):
    width = 512
    for f in range(w1.shape[1] // width):
        cols = slice(f * width, (f + 1) * width)
        half = 0.5 * dot(rows, w1[:, cols])
        hid[:, cols] = (half + half * jnp.tanh(half)).astype(BF)


def step_kernel(
    nc,
    grid_hbm, gown_hbm, gw_hbm, mown_hbm, mw_hbm, feat_hbm, neigh_hbm,
    ew1_hbm, ew2_hbm, gain_hbm, wqkv_hbm, wout_hbm, dw1_hbm, dw2_hbm,
    dec_hbm, mesh_hbm,
    x, enc, res, feat, state, nall, mesh, hid, qt, sel,
    ew1, ew2, wqkv, wout, dw1, dw2, gain, gw, mw, gwt, mwt,
    psend, precv, gown, mown, neigh, *rest,
):
    cands = rest[:nc]
    lsem, osem, s1, r1, s2, r2, s3, r3 = rest[nc:]
    nb, rows, depth = x.shape
    heads = depth // HD
    r = rows // nc
    m = nb * r
    tiles = lax.axis_size("tile")
    count = tiles * lax.axis_size("sub")
    me = lax.axis_index("tile") * lax.axis_size("sub") + lax.axis_index("sub")

    def place(delta):
        d = lax.rem(me + delta + count, count)
        return (d // 2, lax.rem(d, 2))

    loads = {}

    def load(name, src, dst):
        c = pltpu.make_async_copy(src, dst, lsem.at[len(loads)])
        c.start()
        loads[name] = c

    load("gown", gown_hbm, gown)
    load("gw", gw_hbm, gw)
    load("mown", mown_hbm, mown)
    load("mw", mw_hbm, mw)
    load("neigh", neigh_hbm, neigh)
    load("gain", gain_hbm, gain)
    load("x0", grid_hbm.at[:, 0:r, :], x.at[:, 0:r, :])
    load("ew1", ew1_hbm, ew1)
    load("ew2", ew2_hbm, ew2)
    for c in range(1, nc):
        load(f"x{c}", grid_hbm.at[:, c * r:(c + 1) * r, :], x.at[:, c * r:(c + 1) * r, :])
    load("feat", feat_hbm, feat)
    load("wqkv", wqkv_hbm.at[0], wqkv)
    load("wout", wout_hbm.at[0], wout)
    load("dw1", dw1_hbm, dw1)
    load("dw2", dw2_hbm, dw2)

    barrier = pltpu.get_barrier_semaphore()
    for delta in DELTAS:
        pl.semaphore_signal(
            barrier, inc=1, device_id=place(delta), device_id_type=pl.DeviceIdType.MESH
        )

    for name in ("gown", "gw", "mown", "mw", "neigh"):
        loads[name].wait()
    gwt[...] = jnp.tile(gw[...], (rows // nb, 1)).T
    mwt[...] = jnp.tile(mw[...], (rows // nb, 1)).T

    out_row = lax.broadcasted_iota(jnp.int32, (r, r), 0)
    in_row = lax.broadcasted_iota(jnp.int32, (r, r), 1)
    same = (out_row == in_row).astype(F32)
    for b in range(nb):
        e = lax.rem(gown[b] - me + 2 + count, count)
        for s in range(5):
            hit = jnp.where(e == s, 1.0, 0.0).astype(F32)
            sel[s * r:(s + 1) * r, b * r:(b + 1) * r] = (same * hit).astype(BF)

    pl.semaphore_wait(barrier, len(DELTAS))

    def remote(src, dst, ssem, rsem, delta):
        return pltpu.make_async_remote_copy(
            src_ref=src, dst_ref=dst, send_sem=ssem, recv_sem=rsem,
            device_id=place(delta), device_id_type=pl.DeviceIdType.MESH,
        )

    sent = []
    first = {}
    second = {}
    third = {}

    def absorb(c):
        lo, hi = c * r, (c + 1) * r
        total = state[lo:hi, :]
        for k in range(len(DELTAS)):
            first[c, k].wait_recv()
            total = total + precv[c, k].astype(F32)
        state[lo:hi, :] = total
        mean_sq = jnp.mean(total * total, axis=-1, keepdims=True)
        nall[2, lo:hi, :] = (total * lax.rsqrt(mean_sq + 1e-06) * gain[...]).astype(BF)
        for k, delta in enumerate(DELTAS):
            copy = remote(
                nall.at[2, lo:hi, :], nall.at[2 - delta, lo:hi, :],
                s2.at[c, k], r2.at[c, k], delta,
            )
            copy.start()
            second[c, k] = copy
            sent.append(copy)

    lag = 2
    for c in range(nc):
        lo, hi = c * r, (c + 1) * r
        loads[f"x{c}"].wait()
        if c == 0:
            loads["ew1"].wait()
        xb = x[:, lo:hi, :].reshape(m, depth)
        hidden_layer(xb, ew1, hid)
        if c == 0:
            loads["ew2"].wait()
        wcol = jnp.concatenate([gwt[lo:hi, b:b + 1] for b in range(nb)], axis=0)
        pieces = []
        for g in range(0, depth, 256):
            cols = slice(g, g + 256)
            y = xb[:, cols].astype(F32) + dot(hid[...], ew2[:, cols])
            enc[:, lo:hi, cols] = y.astype(BF).reshape(nb, r, 256)
            pieces.append(dot(sel[...], (y * wcol).astype(BF)))
        part = jnp.concatenate(pieces, axis=1)
        if c == 0:
            loads["feat"].wait()
            loads["gain"].wait()
        state[lo:hi, :] = feat[lo:hi, :].astype(F32) + part[2 * r:3 * r]
        for k, delta in enumerate(DELTAS):
            psend[c, k] = part[(2 + delta) * r:(3 + delta) * r].astype(BF)
            copy = remote(psend.at[c, k], precv.at[c, k], s1.at[c, k], r1.at[c, k], delta)
            copy.start()
            first[c, k] = copy
            sent.append(copy)
        if c >= lag:
            absorb(c - lag)
    for c in range(nc - lag, nc):
        absorb(c)

    loads["wqkv"].wait()
    loads["wout"].wait()
    parts = 2
    ar = rows // parts
    q = dot(nall[2], wqkv[:, :depth]).astype(BF)
    for h in range(heads):
        t = lax.dot_general(
            q[:, h * HD:(h + 1) * HD], wqkv[:, depth + h * HD:depth + (h + 1) * HD],
            NT, preferred_element_type=F32,
        ).astype(BF)
        for p in range(parts):
            qt[p, h * ar:(h + 1) * ar, :] = t[p * ar:(p + 1) * ar]
    bias = []
    for s in range(5):
        listed = jnp.int32(0)
        for j in range(3):
            e = lax.rem(neigh[0, j] - me + 2 + count, count)
            listed = listed + jnp.where(e == s, 1, 0)
        bias.append(jnp.where(listed > 0, 0.0, NEG).astype(F32) if s != 2 else None)

    for c in range(nc):
        for k in range(len(DELTAS)):
            second[c, k].wait_recv()

    scale = HD ** -0.5
    per = nc // parts
    for p in range(parts):
        scores = [
            lax.dot_general(qt[p], nall[s], NT, preferred_element_type=F32) * scale
            for s in range(5)
        ]
        scores = [t if s == 2 else t + bias[s] for s, t in enumerate(scores)]
        scores = jnp.concatenate(scores, axis=1)
        top = jnp.max(scores, axis=-1, keepdims=True)
        e = jnp.exp(scores - top)
        total = jnp.sum(e, axis=-1, keepdims=True)
        mixed = dot(e.astype(BF), nall[...].reshape(5 * rows, depth))
        mixed = (mixed / total).astype(BF)
        att = jnp.concatenate([
            dot(
                mixed[h * ar:(h + 1) * ar],
                wqkv[:, 2 * depth + h * HD:2 * depth + (h + 1) * HD],
            ).astype(BF)
            for h in range(heads)
        ], axis=1)
        new = (state[p * ar:(p + 1) * ar, :] + dot(att, wout[...])).astype(BF)
        mesh[p * ar:(p + 1) * ar, :] = new
        for i in range(per):
            c = p * per + i
            cand = cands[c]
            cand[2] = new[i * r:(i + 1) * r]
            for k, delta in enumerate(DELTAS):
                copy = remote(
                    cand.at[2], cand.at[2 - delta], s3.at[c, k], r3.at[c, k], delta
                )
                copy.start()
                third[c, k] = copy
                sent.append(copy)

    outs = [pltpu.make_async_copy(mesh, mesh_hbm, osem.at[nc])]
    outs[0].start()
    loads["dw1"].wait()
    loads["dw2"].wait()
    for c in range(nc):
        lo, hi = c * r, (c + 1) * r
        for k in range(len(DELTAS)):
            third[c, k].wait_recv()
        pieces = []
        for b in range(nb):
            e = jnp.minimum(lax.rem(mown[b] - me + 2 + count, count), 4)
            pieces.append(
                enc[b, lo:hi, :].astype(F32)
                + mwt[lo:hi, b:b + 1] * cands[c][e].astype(F32)
            )
        rows_in = jnp.concatenate(pieces, axis=0).astype(BF)
        hidden_layer(rows_in, dw1, hid)
        for g in range(0, depth, 256):
            cols = slice(g, g + 256)
            y = rows_in[:, cols].astype(F32) + dot(hid[...], dw2[:, cols])
            res[:, lo:hi, cols] = y.astype(BF).reshape(nb, r, 256)
        out = pltpu.make_async_copy(
            res.at[:, lo:hi, :], dec_hbm.at[:, lo:hi, :], osem.at[c]
        )
        out.start()
        outs.append(out)
    for copy in sent:
        copy.wait_send()
    for out in outs:
        out.wait()


def on_device(
    grid, g2m_owner, g2m_weight, m2g_owner, m2g_weight, mesh_feat, neighbours,
    enc_w1, enc_w2, attn_gain, w_qkv, w_out, dec_w1, dec_w2,
):
    nb = g2m_owner.shape[0]
    rows, depth = mesh_feat.shape
    ff = enc_w1.shape[1]
    nc = 4
    r = rows // nc
    nd = len(DELTAS)
    any_spec = pl.BlockSpec(memory_space=pl.ANY)
    dma = pltpu.SemaphoreType.DMA
    vm = pltpu.VMEM
    decoded, mesh_out = pl.pallas_call(
        functools.partial(step_kernel, nc),
        out_shape=(
            jax.ShapeDtypeStruct((nb, rows, depth), BF),
            jax.ShapeDtypeStruct((rows, depth), BF),
        ),
        in_specs=[any_spec] * 14,
        out_specs=(any_spec, any_spec),
        scratch_shapes=[
            vm((nb, rows, depth), BF),
            vm((nb, rows, depth), BF),
            vm((nb, rows, depth), BF),
            vm((rows, depth), BF),
            vm((rows, depth), F32),
            vm((5, rows, depth), BF),
            vm((rows, depth), BF),
            vm((nb * r, ff), BF),
            vm((2, rows // 2 * (depth // HD), depth), BF),
            vm((5 * r, nb * r), BF),
            vm((depth, ff), BF),
            vm((ff, depth), BF),
            vm((depth, 3 * depth), BF),
            vm((depth, depth), BF),
            vm((depth, ff), BF),
            vm((ff, depth), BF),
            vm((1, depth), F32),
            vm((nb, rows), F32),
            vm((nb, rows), F32),
            vm((rows, rows), F32),
            vm((rows, rows), F32),
            vm((nc, nd, r, depth), BF),
            vm((nc, nd, r, depth), BF),
            pltpu.SMEM((nb,), jnp.int32),
            pltpu.SMEM((nb,), jnp.int32),
            pltpu.SMEM((1, 3), jnp.int32),
        ]
        + [vm((5, r, depth), BF)] * nc
        + [dma((20,)), dma((nc + 1,))]
        + [dma((nc, nd))] * 6,
        compiler_params=pltpu.CompilerParams(
            collective_id=0, has_side_effects=True, vmem_limit_bytes=60000 * 1024
        ),
        name="step",
    )(
        grid.reshape(nb, rows, depth), g2m_owner, g2m_weight.reshape(nb, rows),
        m2g_owner, m2g_weight.reshape(nb, rows), mesh_feat, neighbours,
        enc_w1, enc_w2, attn_gain, w_qkv, w_out, dec_w1, dec_w2,
    )
    return decoded.reshape(nb * rows, depth), mesh_out


def solution(mesh):
    cut = P(("tile", "sub"))
    cut2 = P(("tile", "sub"), None)
    in_specs = (cut2, cut, cut, cut, cut, cut2, cut2) + (P(),) * 7
    return jax.shard_map(
        on_device, mesh=mesh, in_specs=in_specs, out_specs=(cut2, cut2), check_vma=False
    )
```

```python
import functools

import jax
import jax.numpy as jnp
from jax import lax
from jax.experimental import pallas as pl
from jax.experimental.pallas import tpu as pltpu
from jax.sharding import PartitionSpec as P

HD = 128
DELTAS = (-2, 2, -1, 1)
SLOT = {-2: 0, -1: 1, 1: 2, 2: 3}
OWN = 4
CHUNKS = 4
LAG = 2
NEG = -1e30
BF = jnp.bfloat16
F32 = jnp.float32
NT = (((1,), (1,)), ((), ()))


def dot(a, b):
    return jnp.dot(a, b, preferred_element_type=F32)


def dot_nt(a, b):
    return lax.dot_general(a, b, NT, preferred_element_type=F32)


def hidden_layer(rows, w1, hid):
    width = 512
    for f in range(w1.shape[1] // width):
        cols = slice(f * width, (f + 1) * width)
        half = 0.5 * dot(rows, w1[:, cols])
        hid[:, cols] = (half + half * jnp.tanh(half)).astype(BF)


def step_kernel(
    grid_hbm, gown_hbm, gw_hbm, mown_hbm, mw_hbm, feat_hbm, neigh_hbm,
    ew1_hbm, ew2_hbm, gain_hbm, wqkv_hbm, wout_hbm, dw1_hbm, dw2_hbm,
    res, rin, mesh, dw1, dw2,
    x, enc, feat, state, nall, hid, qt, sown, bias, wvo, sel,
    ew1, ew2, wqkv, wout, gain, gw, mw, gwt, mwt,
    psend, precv, gown, mown, neigh, *rest,
):
    nc = CHUNKS
    cands = rest[:nc]
    lsem, s1, r1, s2, r2, s3, r3 = rest[nc:]
    nb, rows, depth = x.shape
    heads = depth // HD
    r = rows // nc
    m = nb * r
    count = lax.axis_size("tile") * lax.axis_size("sub")
    me = lax.axis_index("tile") * lax.axis_size("sub") + lax.axis_index("sub")

    def place(delta):
        d = lax.rem(me + delta + count, count)
        return (d // 2, lax.rem(d, 2))

    def offset(block):
        return lax.rem(block - me + 2 + count, count)

    barrier = pltpu.get_barrier_semaphore()
    for delta in DELTAS:
        pl.semaphore_signal(
            barrier, inc=1, device_id=place(delta), device_id_type=pl.DeviceIdType.MESH
        )

    loads = {}

    def load(name, src, dst):
        c = pltpu.make_async_copy(src, dst, lsem.at[len(loads)])
        c.start()
        loads[name] = c

    load("gown", gown_hbm, gown)
    load("gw", gw_hbm, gw)
    load("mown", mown_hbm, mown)
    load("mw", mw_hbm, mw)
    load("neigh", neigh_hbm, neigh)
    load("gain", gain_hbm, gain)
    load("x0", grid_hbm.at[:, 0:r, :], x.at[:, 0:r, :])
    load("ew1", ew1_hbm, ew1)
    load("ew2", ew2_hbm, ew2)
    for c in range(1, nc):
        load(f"x{c}", grid_hbm.at[:, c * r:(c + 1) * r, :], x.at[:, c * r:(c + 1) * r, :])
    load("feat", feat_hbm, feat)
    load("wqkv", wqkv_hbm.at[0], wqkv)
    load("wout", wout_hbm.at[0], wout)
    load("dw1", dw1_hbm, dw1)
    load("dw2", dw2_hbm, dw2)

    for name in ("gown", "gw", "mown", "mw", "neigh"):
        loads[name].wait()
    gwt[...] = jnp.tile(gw[...], (rows // nb, 1)).T
    mwt[...] = jnp.tile(mw[...], (rows // nb, 1)).T

    out_row = lax.broadcasted_iota(jnp.int32, (r, r), 0)
    in_row = lax.broadcasted_iota(jnp.int32, (r, r), 1)
    same = (out_row == in_row).astype(F32)
    for b in range(nb):
        e = offset(gown[b])
        for s in range(5):
            hit = jnp.where(e == s, 1.0, 0.0).astype(F32)
            sel[s * r:(s + 1) * r, b * r:(b + 1) * r] = (same * hit).astype(BF)
    for delta, s in SLOT.items():
        listed = jnp.int32(0)
        for j in range(3):
            listed = listed + jnp.where(offset(neigh[0, j]) == 2 + delta, 1, 0)
        fill = jnp.where(listed > 0, 0.0, NEG).astype(F32)
        bias[:, s * rows:(s + 1) * rows] = jnp.full((1, rows), fill, F32)

    def remote(src, dst, ssem, rsem, delta):
        return pltpu.make_async_remote_copy(
            src_ref=src, dst_ref=dst, send_sem=ssem, recv_sem=rsem,
            device_id=place(delta), device_id_type=pl.DeviceIdType.MESH,
        )

    sent = []
    first = {}
    second = {}
    third = {}

    def absorb(c):
        lo, hi = c * r, (c + 1) * r
        total = state[lo:hi, :]
        for k in range(len(DELTAS)):
            first[c, k].wait_recv()
            total = total + precv[c, k].astype(F32)
        state[lo:hi, :] = total
        mean_sq = jnp.mean(total * total, axis=-1, keepdims=True)
        nall[OWN, lo:hi, :] = (total * lax.rsqrt(mean_sq + 1e-06) * gain[...]).astype(BF)
        for k, delta in enumerate(DELTAS):
            copy = remote(
                nall.at[OWN, lo:hi, :], nall.at[SLOT[-delta], lo:hi, :],
                s2.at[c, k], r2.at[c, k], delta,
            )
            copy.start()
            second[c, k] = copy
            sent.append(copy)

    for c in range(nc):
        lo, hi = c * r, (c + 1) * r
        loads[f"x{c}"].wait()
        if c == 0:
            loads["ew1"].wait()
        xb = x[:, lo:hi, :].reshape(m, depth)
        hidden_layer(xb, ew1, hid)
        if c == 0:
            loads["ew2"].wait()
        wcol = jnp.concatenate([gwt[lo:hi, b:b + 1] for b in range(nb)], axis=0)
        y = xb.astype(F32) + dot(hid[...], ew2[...])
        enc[:, lo:hi, :] = y.astype(BF).reshape(nb, r, depth)
        part = dot(sel[...], (y * wcol).astype(BF))
        if c == 0:
            loads["feat"].wait()
            loads["gain"].wait()
            pl.semaphore_wait(barrier, len(DELTAS))
        state[lo:hi, :] = feat[lo:hi, :].astype(F32) + part[2 * r:3 * r]
        for k, delta in enumerate(DELTAS):
            psend[c, k] = part[(2 + delta) * r:(3 + delta) * r].astype(BF)
            copy = remote(psend.at[c, k], precv.at[c, k], s1.at[c, k], r1.at[c, k], delta)
            copy.start()
            first[c, k] = copy
            sent.append(copy)
        if c >= LAG:
            absorb(c - LAG)
    for c in range(nc - LAG, nc - 1):
        absorb(c)

    loads["wqkv"].wait()
    loads["wout"].wait()
    for h in range(heads):
        cols = slice(2 * depth + h * HD, 2 * depth + (h + 1) * HD)
        wvo[h * depth:(h + 1) * depth, :] = dot(
            wqkv[:, cols], wout[h * HD:(h + 1) * HD, :]
        ).astype(BF)
    absorb(nc - 1)

    parts = 2
    ar = rows // parts
    scale = HD ** -0.5
    q = dot(nall[OWN], wqkv[:, :depth]).astype(BF)
    for h in range(heads):
        t = scale * dot_nt(
            q[:, h * HD:(h + 1) * HD], wqkv[:, depth + h * HD:depth + (h + 1) * HD]
        )
        for p in range(parts):
            qt[p, h * ar:(h + 1) * ar, :] = t[p * ar:(p + 1) * ar].astype(BF)
    for p in range(parts):
        sown[p] = dot_nt(qt[p], nall[OWN])

    for c in range(nc):
        for k in range(len(DELTAS)):
            second[c, k].wait_recv()

    per = nc // parts
    for p in range(parts):
        scores = dot_nt(qt[p], nall[0:OWN].reshape(OWN * rows, depth)) + bias[...]
        scores = jnp.concatenate([scores, sown[p]], axis=1)
        top = jnp.max(scores, axis=-1, keepdims=True)
        e = jnp.exp(scores - top)
        total = jnp.sum(e, axis=-1, keepdims=True)
        mixed = dot(e.astype(BF), nall[...].reshape(5 * rows, depth))
        mixed = (mixed / total).astype(BF)
        mixed = jnp.concatenate([mixed[h * ar:(h + 1) * ar] for h in range(heads)], axis=1)
        new = (state[p * ar:(p + 1) * ar, :] + dot(mixed, wvo[...])).astype(BF)
        mesh[p * ar:(p + 1) * ar, :] = new
        for i in range(per):
            c = p * per + i
            cand = cands[c]
            cand[2] = new[i * r:(i + 1) * r]
            for k, delta in enumerate(DELTAS):
                copy = remote(
                    cand.at[2], cand.at[2 - delta], s3.at[c, k], r3.at[c, k], delta
                )
                copy.start()
                third[c, k] = copy
                sent.append(copy)

    loads["dw1"].wait()
    loads["dw2"].wait()
    for c in range(nc):
        lo, hi = c * r, (c + 1) * r
        for k in range(len(DELTAS)):
            third[c, k].wait_recv()
        pieces = []
        for b in range(nb):
            e = jnp.minimum(offset(mown[b]), 4)
            pieces.append(
                enc[b, lo:hi, :].astype(F32)
                + mwt[lo:hi, b:b + 1] * cands[c][e].astype(F32)
            )
        rows_in = jnp.concatenate(pieces, axis=0).astype(BF)
        if c == nc - 1:
            rin[...] = rows_in
            break
        hidden_layer(rows_in, dw1, hid)
        y = rows_in.astype(F32) + dot(hid[...], dw2[...])
        res[:, lo:hi, :] = y.astype(BF).reshape(nb, r, depth)
    for copy in sent:
        copy.wait_send()


def last_kernel(res, rin, mesh, dw1, dw2, dec_hbm, mesh_hbm, hid, tail, sem):
    nb, rows, depth = res.shape
    m = rin.shape[0]
    r = m // nb
    done = rows - r
    outs = [
        pltpu.make_async_copy(
            res.at[:, 0:done, :], dec_hbm.at[:, 0:done, :], sem.at[0]
        ),
        pltpu.make_async_copy(mesh, mesh_hbm, sem.at[1]),
    ]
    for out in outs:
        out.start()
    rows_in = rin[...]
    hidden_layer(rows_in, dw1, hid)
    y = rows_in.astype(F32) + dot(hid[...], dw2[...])
    tail[...] = y.astype(BF).reshape(nb, r, depth)
    out = pltpu.make_async_copy(tail, dec_hbm.at[:, done:, :], sem.at[2])
    out.start()
    outs.append(out)
    for out in outs:
        out.wait()


def on_device(
    grid, g2m_owner, g2m_weight, m2g_owner, m2g_weight, mesh_feat, neighbours,
    enc_w1, enc_w2, attn_gain, w_qkv, w_out, dec_w1, dec_w2,
):
    nb = g2m_owner.shape[0]
    rows, depth = mesh_feat.shape
    ff = enc_w1.shape[1]
    nc = CHUNKS
    r = rows // nc
    nd = len(DELTAS)
    heads = depth // HD
    any_spec = pl.BlockSpec(memory_space=pl.ANY)
    vm_spec = pl.BlockSpec(memory_space=pltpu.VMEM)
    dma = pltpu.SemaphoreType.DMA
    vm = pltpu.VMEM
    held = pl.pallas_call(
        step_kernel,
        out_shape=(
            vm((nb, rows, depth), BF),
            vm((nb * r, depth), BF),
            vm((rows, depth), BF),
            vm((depth, ff), BF),
            vm((ff, depth), BF),
        ),
        in_specs=[pl.BlockSpec(memory_space=pltpu.HBM)] * 14,
        out_specs=(vm_spec,) * 5,
        scratch_shapes=[
            vm((nb, rows, depth), BF),
            vm((nb, rows, depth), BF),
            vm((rows, depth), BF),
            vm((rows, depth), F32),
            vm((5, rows, depth), BF),
            vm((nb * r, ff), BF),
            vm((2, rows // 2 * heads, depth), BF),
            vm((2, rows // 2 * heads, rows), F32),
            vm((1, OWN * rows), F32),
            vm((heads * depth, depth), BF),
            vm((5 * r, nb * r), BF),
            vm((depth, ff), BF),
            vm((ff, depth), BF),
            vm((depth, 3 * depth), BF),
            vm((depth, depth), BF),
            vm((1, depth), F32),
            vm((nb, rows), F32),
            vm((nb, rows), F32),
            vm((rows, rows), F32),
            vm((rows, rows), F32),
            vm((nc, nd, r, depth), BF),
            vm((nc, nd, r, depth), BF),
            pltpu.SMEM((nb,), jnp.int32),
            pltpu.SMEM((nb,), jnp.int32),
            pltpu.SMEM((1, 3), jnp.int32),
        ]
        + [vm((5, r, depth), BF)] * nc
        + [dma((20,))]
        + [dma((nc, nd))] * 6,
        compiler_params=pltpu.CompilerParams(
            collective_id=0, has_side_effects=True, vmem_limit_bytes=40 * 2**20
        ),
        name="step",
    )(*[pltpu.with_memory_space_constraint(a, pltpu.HBM) for a in (
        grid.reshape(nb, rows, depth), g2m_owner, g2m_weight.reshape(nb, rows),
        m2g_owner, m2g_weight.reshape(nb, rows), mesh_feat, neighbours,
        enc_w1, enc_w2, attn_gain, w_qkv, w_out, dec_w1, dec_w2,
    )])
    decoded, mesh_out = pl.pallas_call(
        last_kernel,
        out_shape=(
            jax.ShapeDtypeStruct((nb, rows, depth), BF),
            jax.ShapeDtypeStruct((rows, depth), BF),
        ),
        in_specs=[vm_spec] * 5,
        out_specs=(any_spec, any_spec),
        scratch_shapes=[
            vm((nb * r, ff), BF),
            vm((nb, r, depth), BF),
            dma((3,)),
        ],
        compiler_params=pltpu.CompilerParams(vmem_limit_bytes=16 * 2**20),
        name="last",
    )(*[pltpu.with_memory_space_constraint(a, pltpu.VMEM) for a in held])
    return decoded.reshape(nb * rows, depth), mesh_out


def solution(mesh):
    cut = P(("tile", "sub"))
    cut2 = P(("tile", "sub"), None)
    in_specs = (cut2, cut, cut, cut, cut, cut2, cut2) + (P(),) * 7
    return jax.shard_map(
        on_device, mesh=mesh, in_specs=in_specs, out_specs=(cut2, cut2), check_vma=False
    )
```

```python
import functools

import jax
import jax.numpy as jnp
from jax import lax
from jax.experimental import pallas as pl
from jax.experimental.pallas import tpu as pltpu
from jax.sharding import PartitionSpec as P

HD = 128
DELTAS = (-2, 2, -1, 1)
SLOT = {-2: 0, -1: 1, 1: 2, 2: 3}
OWN = 4
CHUNKS = 4
LAG = 2
NEG = -1e30
PLANE = 32
EDGES = (
    (0, (-2, -1), 1, -1),
    (1, (-2,), -1, -2),
    (PLANE - 2, (2,), 1, 2),
    (PLANE - 1, (1, 2), -1, 1),
)
BF = jnp.bfloat16
F32 = jnp.float32
NT = (((1,), (1,)), ((), ()))


def dot(a, b):
    return jnp.dot(a, b, preferred_element_type=F32)


def dot_nt(a, b):
    return lax.dot_general(a, b, NT, preferred_element_type=F32)


def hidden_layer(rows, w1, hid, ready=lambda f: None):
    width = 512
    for f in range(0, w1.shape[1], width):
        ready(f)
        cols = slice(f, f + width)
        half = 0.5 * dot(rows, w1[:, cols])
        hid[:, cols] = (half + half * jnp.tanh(half)).astype(BF)


def step_kernel(
    grid_hbm, gown_hbm, gw_hbm, mown_hbm, mw_hbm, feat_hbm, neigh_hbm,
    ew1_hbm, ew2_hbm, gain_hbm, wqkv_hbm, wout_hbm, dw1_hbm, dw2_hbm,
    res, rin, mesh, dw1, dw2,
    x, enc, feat, state, nall, hid, qt, sown, bias, wvo, sel,
    ew1, ew2, wqkv, wout, gain, gw, mw, gwt, mwt,
    psend, precv, wy, asend, arecv, xrecv, gown, mown, neigh, *rest,
):
    nc = CHUNKS
    cands = rest[:nc]
    lsem, s1, r1, s2, r2, s3, r3, sx, rx = rest[nc:]
    nb, rows, depth = x.shape
    heads = depth // HD
    r = rows // nc
    m = nb * r
    count = lax.axis_size("tile") * lax.axis_size("sub")
    me = lax.axis_index("tile") * lax.axis_size("sub") + lax.axis_index("sub")

    def place(delta):
        d = lax.rem(me + delta + count, count)
        return (d // 2, lax.rem(d, 2))

    def offset(block):
        return lax.rem(block - me + 2 + count, count)

    barrier = pltpu.get_barrier_semaphore()
    for delta in DELTAS:
        pl.semaphore_signal(
            barrier, inc=1, device_id=place(delta), device_id_type=pl.DeviceIdType.MESH
        )

    loads = {}

    def load(name, src, dst):
        c = pltpu.make_async_copy(src, dst, lsem.at[len(loads)])
        c.start()
        loads[name] = c

    load("gown", gown_hbm, gown)
    load("gw", gw_hbm, gw)
    load("mown", mown_hbm, mown)
    load("mw", mw_hbm, mw)
    load("neigh", neigh_hbm, neigh)
    load("gain", gain_hbm, gain)
    load("x0", grid_hbm.at[:, 0:r, :], x.at[:, 0:r, :])
    width = 512
    ff = ew1.shape[1]
    for f in range(0, ff, width):
        load(f"ew1_{f}", ew1_hbm.at[:, f:f + width], ew1.at[:, f:f + width])
    load("ew2", ew2_hbm, ew2)
    for c in range(1, nc):
        load(f"x{c}", grid_hbm.at[:, c * r:(c + 1) * r, :], x.at[:, c * r:(c + 1) * r, :])
    load("feat", feat_hbm, feat)
    load("wqkv", wqkv_hbm.at[0], wqkv)
    load("wout", wout_hbm.at[0], wout)
    load("dw1", dw1_hbm, dw1)
    load("dw2", dw2_hbm, dw2)

    for name in ("gown", "gw", "mown", "mw", "neigh"):
        loads[name].wait()
    gwt[...] = jnp.tile(gw[...], (rows // nb, 1)).T
    mwt[...] = jnp.tile(mw[...], (rows // nb, 1)).T

    out_row = lax.broadcasted_iota(jnp.int32, (r, r), 0)
    in_row = lax.broadcasted_iota(jnp.int32, (r, r), 1)
    same = (out_row == in_row).astype(F32)
    for b in range(nb):
        e = offset(gown[b])
        for s in range(5):
            hit = jnp.where(e == s, 1.0, 0.0).astype(F32)
            sel[s * r:(s + 1) * r, b * r:(b + 1) * r] = (same * hit).astype(BF)
    for delta, s in SLOT.items():
        listed = jnp.int32(0)
        for j in range(3):
            listed = listed + jnp.where(offset(neigh[0, j]) == 2 + delta, 1, 0)
        fill = jnp.where(listed > 0, 0.0, NEG).astype(F32)
        bias[:, s * rows:(s + 1) * rows] = jnp.full((1, rows), fill, F32)

    def remote(src, dst, ssem, rsem, delta):
        return pltpu.make_async_remote_copy(
            src_ref=src, dst_ref=dst, send_sem=ssem, recv_sem=rsem,
            device_id=place(delta), device_id_type=pl.DeviceIdType.MESH,
        )

    def spot(c):
        return slice(c * r, (c + 1) * r)

    def first(c, delta):
        k = SLOT[delta]
        return remote(psend.at[c, k], precv.at[c, k], s1.at[c, k], r1.at[c, k], delta)

    def second(c, delta):
        k = SLOT[delta]
        return remote(
            nall.at[OWN, spot(c), :], nall.at[SLOT[-delta], spot(c), :],
            s2.at[c, k], r2.at[c, k], delta,
        )

    def across(c, delta):
        k = SLOT[delta]
        return remote(asend.at[c], arecv.at[c, k], s2.at[c, k], r2.at[c, k], delta)

    def shared(c, partner, target):
        return remote(psend.at[c, SLOT[target]], xrecv.at[c], sx.at[c], rx.at[c], partner)

    def third(c, delta):
        k = SLOT[delta]
        cand = cands[c]
        return remote(cand.at[2], cand.at[2 - delta], s3.at[c, k], r3.at[c, k], delta)

    place_in_plane = lax.rem(me, PLANE)
    inner = jnp.logical_and(place_in_plane > 1, place_in_plane < PLANE - 2)

    def add(c, total, sources):
        for source in sources:
            first(c, -source).wait_recv()
            total = total + precv[c, SLOT[-source]].astype(F32)
        return total

    def norm(total):
        mean_sq = jnp.mean(total * total, axis=-1, keepdims=True)
        return (total * lax.rsqrt(mean_sq + 1e-06) * gain[...]).astype(BF)

    def finish(c, sources, targets):
        total = add(c, state[spot(c), :], sources)
        state[spot(c), :] = total
        nall[OWN, spot(c), :] = norm(total)
        for delta in targets:
            second(c, delta).start()

    def presum(c):
        for q, cross, _, _ in EDGES:
            @pl.when(place_in_plane == q)
            def _(cross=cross):
                total = add(c, state[spot(c), :], [d for d in DELTAS if d not in cross])
                state[spot(c), :] = total
                asend[c] = total.astype(BF)
                for delta in cross:
                    across(c, delta).start()

    def absorb(c):
        @pl.when(inner)
        def _():
            finish(c, DELTAS, DELTAS)

        presum(c)

    def contribute(c):
        part = dot(sel[...], wy[...])
        if c == 0:
            loads["feat"].wait()
            loads["gain"].wait()
            pl.semaphore_wait(barrier, len(DELTAS))
        state[spot(c), :] = feat[spot(c), :].astype(F32) + part[2 * r:3 * r]
        for delta in DELTAS:
            psend[c, SLOT[delta]] = part[(2 + delta) * r:(3 + delta) * r].astype(BF)
            first(c, delta).start()
        for q, _, partner, target in EDGES:
            @pl.when(place_in_plane == q)
            def _(partner=partner, target=target):
                shared(c, partner, target).start()

    for c in range(nc):
        loads[f"x{c}"].wait()
        xb = x[:, spot(c), :].reshape(m, depth)
        hidden_layer(xb, ew1, hid, lambda f, c=c: c == 0 and loads[f"ew1_{f}"].wait())
        if c > 0:
            contribute(c - 1)
        if c == 0:
            loads["ew2"].wait()
        wcol = jnp.concatenate([gwt[spot(c), b:b + 1] for b in range(nb)], axis=0)
        y = xb.astype(F32) + dot(hid[...], ew2[...])
        enc[:, spot(c), :] = y.astype(BF).reshape(nb, r, depth)
        wy[...] = (y * wcol).astype(BF)
        if c >= LAG:
            absorb(c - LAG)
    contribute(nc - 1)
    for c in range(nc - LAG, nc - 1):
        absorb(c)

    loads["wqkv"].wait()
    loads["wout"].wait()
    for h in range(heads):
        cols = slice(2 * depth + h * HD, 2 * depth + (h + 1) * HD)
        wvo[h * depth:(h + 1) * depth, :] = dot(
            wqkv[:, cols], wout[h * HD:(h + 1) * HD, :]
        ).astype(BF)
    absorb(nc - 1)
    for q, cross, _, _ in EDGES:
        @pl.when(place_in_plane == q)
        def _(cross=cross):
            for c in range(nc):
                finish(c, cross, [d for d in DELTAS if d not in cross])

    parts = 2
    ar = rows // parts
    scale = HD ** -0.5
    q = dot(nall[OWN], wqkv[:, :depth]).astype(BF)
    for h in range(heads):
        t = scale * dot_nt(
            q[:, h * HD:(h + 1) * HD], wqkv[:, depth + h * HD:depth + (h + 1) * HD]
        )
        for p in range(parts):
            qt[p, h * ar:(h + 1) * ar, :] = t[p * ar:(p + 1) * ar].astype(BF)
    for p in range(parts):
        sown[p] = dot_nt(qt[p], nall[OWN])

    @pl.when(inner)
    def _():
        for c in range(nc):
            for delta in DELTAS:
                second(c, delta).wait_recv()

    for q, cross, partner, target in EDGES:
        @pl.when(place_in_plane == q)
        def _(cross=cross, partner=partner, target=target):
            for c in range(nc):
                for source in DELTAS:
                    if source not in cross:
                        second(c, -source).wait_recv()
                shared(c, partner, target).wait_recv()
                for source in cross:
                    across(c, -source).wait_recv()
                    total = arecv[c, SLOT[-source]].astype(F32)
                    total = total + psend[c, SLOT[source]].astype(F32)
                    if source == target:
                        total = total + xrecv[c].astype(F32)
                    nall[SLOT[source], spot(c), :] = norm(total)

    per = nc // parts
    for p in range(parts):
        scores = dot_nt(qt[p], nall[0:OWN].reshape(OWN * rows, depth)) + bias[...]
        scores = jnp.concatenate([scores, sown[p]], axis=1)
        top = jnp.max(scores, axis=-1, keepdims=True)
        e = jnp.exp(scores - top)
        total = jnp.sum(e, axis=-1, keepdims=True)
        mixed = dot(e.astype(BF), nall[...].reshape(5 * rows, depth))
        mixed = (mixed / total).astype(BF)
        mixed = jnp.concatenate([mixed[h * ar:(h + 1) * ar] for h in range(heads)], axis=1)
        new = (state[p * ar:(p + 1) * ar, :] + dot(mixed, wvo[...])).astype(BF)
        mesh[p * ar:(p + 1) * ar, :] = new
        for i in range(per):
            c = p * per + i
            cands[c][2] = new[i * r:(i + 1) * r]
            for delta in DELTAS:
                third(c, delta).start()

    loads["dw1"].wait()
    loads["dw2"].wait()
    for c in range(nc):
        lo, hi = c * r, (c + 1) * r
        for delta in DELTAS:
            third(c, delta).wait_recv()
        pieces = []
        for b in range(nb):
            e = jnp.minimum(offset(mown[b]), 4)
            pieces.append(
                enc[b, lo:hi, :].astype(F32)
                + mwt[lo:hi, b:b + 1] * cands[c][e].astype(F32)
            )
        rows_in = jnp.concatenate(pieces, axis=0).astype(BF)
        if c == nc - 1:
            rin[...] = rows_in
            break
        hidden_layer(rows_in, dw1, hid)
        y = rows_in.astype(F32) + dot(hid[...], dw2[...])
        res[:, lo:hi, :] = y.astype(BF).reshape(nb, r, depth)
    for c in range(nc):
        for delta in DELTAS:
            first(c, delta).wait_send()
            third(c, delta).wait_send()

    @pl.when(inner)
    def _():
        for c in range(nc):
            for delta in DELTAS:
                second(c, delta).wait_send()

    for q, cross, partner, target in EDGES:
        @pl.when(place_in_plane == q)
        def _(cross=cross, partner=partner, target=target):
            for c in range(nc):
                shared(c, partner, target).wait_send()
                for delta in DELTAS:
                    if delta in cross:
                        across(c, delta).wait_send()
                    else:
                        second(c, delta).wait_send()


def last_kernel(res, rin, mesh, dw1, dw2, dec_hbm, mesh_hbm, hid, tail, sem):
    nb, rows, depth = res.shape
    m = rin.shape[0]
    r = m // nb
    done = rows - r
    outs = [
        pltpu.make_async_copy(
            res.at[:, 0:done, :], dec_hbm.at[:, 0:done, :], sem.at[0]
        ),
        pltpu.make_async_copy(mesh, mesh_hbm, sem.at[1]),
    ]
    for out in outs:
        out.start()
    rows_in = rin[...]
    hidden_layer(rows_in, dw1, hid)
    y = rows_in.astype(F32) + dot(hid[...], dw2[...])
    tail[...] = y.astype(BF).reshape(nb, r, depth)
    out = pltpu.make_async_copy(tail, dec_hbm.at[:, done:, :], sem.at[2])
    out.start()
    outs.append(out)
    for out in outs:
        out.wait()


def on_device(
    grid, g2m_owner, g2m_weight, m2g_owner, m2g_weight, mesh_feat, neighbours,
    enc_w1, enc_w2, attn_gain, w_qkv, w_out, dec_w1, dec_w2,
):
    nb = g2m_owner.shape[0]
    rows, depth = mesh_feat.shape
    ff = enc_w1.shape[1]
    nc = CHUNKS
    r = rows // nc
    nd = len(DELTAS)
    heads = depth // HD
    any_spec = pl.BlockSpec(memory_space=pl.ANY)
    vm_spec = pl.BlockSpec(memory_space=pltpu.VMEM)
    dma = pltpu.SemaphoreType.DMA
    vm = pltpu.VMEM
    held = pl.pallas_call(
        step_kernel,
        out_shape=(
            vm((nb, rows, depth), BF),
            vm((nb * r, depth), BF),
            vm((rows, depth), BF),
            vm((depth, ff), BF),
            vm((ff, depth), BF),
        ),
        in_specs=[pl.BlockSpec(memory_space=pltpu.HBM)] * 14,
        out_specs=(vm_spec,) * 5,
        scratch_shapes=[
            vm((nb, rows, depth), BF),
            vm((nb, rows, depth), BF),
            vm((rows, depth), BF),
            vm((rows, depth), F32),
            vm((5, rows, depth), BF),
            vm((nb * r, ff), BF),
            vm((2, rows // 2 * heads, depth), BF),
            vm((2, rows // 2 * heads, rows), F32),
            vm((1, OWN * rows), F32),
            vm((heads * depth, depth), BF),
            vm((5 * r, nb * r), BF),
            vm((depth, ff), BF),
            vm((ff, depth), BF),
            vm((depth, 3 * depth), BF),
            vm((depth, depth), BF),
            vm((1, depth), F32),
            vm((nb, rows), F32),
            vm((nb, rows), F32),
            vm((rows, rows), F32),
            vm((rows, rows), F32),
            vm((nc, nd, r, depth), BF),
            vm((nc, nd, r, depth), BF),
            vm((nb * r, depth), BF),
            vm((nc, r, depth), BF),
            vm((nc, nd, r, depth), BF),
            vm((nc, r, depth), BF),
            pltpu.SMEM((nb,), jnp.int32),
            pltpu.SMEM((nb,), jnp.int32),
            pltpu.SMEM((1, 3), jnp.int32),
        ]
        + [vm((5, r, depth), BF)] * nc
        + [dma((24,))]
        + [dma((nc, nd))] * 6
        + [dma((nc,))] * 2,
        compiler_params=pltpu.CompilerParams(
            collective_id=0, has_side_effects=True, vmem_limit_bytes=40 * 2**20
        ),
        name="step",
    )(*[pltpu.with_memory_space_constraint(a, pltpu.HBM) for a in (
        grid.reshape(nb, rows, depth), g2m_owner, g2m_weight.reshape(nb, rows),
        m2g_owner, m2g_weight.reshape(nb, rows), mesh_feat, neighbours,
        enc_w1, enc_w2, attn_gain, w_qkv, w_out, dec_w1, dec_w2,
    )])
    decoded, mesh_out = pl.pallas_call(
        last_kernel,
        out_shape=(
            jax.ShapeDtypeStruct((nb, rows, depth), BF),
            jax.ShapeDtypeStruct((rows, depth), BF),
        ),
        in_specs=[vm_spec] * 5,
        out_specs=(any_spec, any_spec),
        scratch_shapes=[
            vm((nb * r, ff), BF),
            vm((nb, r, depth), BF),
            dma((3,)),
        ],
        compiler_params=pltpu.CompilerParams(vmem_limit_bytes=16 * 2**20),
        name="last",
    )(*[pltpu.with_memory_space_constraint(a, pltpu.VMEM) for a in held])
    return decoded.reshape(nb * rows, depth), mesh_out


def solution(mesh):
    cut = P(("tile", "sub"))
    cut2 = P(("tile", "sub"), None)
    in_specs = (cut2, cut, cut, cut, cut, cut2, cut2) + (P(),) * 7
    return jax.shard_map(
        on_device, mesh=mesh, in_specs=in_specs, out_specs=(cut2, cut2), check_vma=False
    )
```

```python
import functools

import jax
import jax.numpy as jnp
from jax import lax
from jax.experimental import pallas as pl
from jax.experimental.pallas import tpu as pltpu
from jax.sharding import PartitionSpec as P

HD = 128
DELTAS = (-2, 2, -1, 1)
SLOT = {-2: 0, -1: 1, 1: 2, 2: 3}
OWN = 4
CHUNKS = 4
LAG = 2
NEG = -1e30
PLANE = 32
EDGES = (
    (0, (-2, -1), 1, -1),
    (1, (-2,), -1, -2),
    (PLANE - 2, (2,), 1, 2),
    (PLANE - 1, (1, 2), -1, 1),
)
BF = jnp.bfloat16
F32 = jnp.float32
NT = (((1,), (1,)), ((), ()))


def dot(a, b):
    return jnp.dot(a, b, preferred_element_type=F32)


def dot_nt(a, b):
    return lax.dot_general(a, b, NT, preferred_element_type=F32)


def crosses_up(position, delta):
    if delta < 0:
        return jnp.bool_(False)
    return jnp.logical_and(position < PLANE, position + delta >= PLANE)


def hidden_layer(rows, w1, hid, ready=lambda f: None):
    width = 512
    for f in range(0, w1.shape[1], width):
        ready(f)
        cols = slice(f, f + width)
        half = 0.5 * dot(rows, w1[:, cols])
        hid[:, cols] = (half + half * jnp.tanh(half)).astype(BF)


def step_kernel(
    grid_hbm, gown_hbm, gw_hbm, mown_hbm, mw_hbm, feat_hbm, neigh_hbm,
    ew1_hbm, ew2_hbm, gain_hbm, wqkv_hbm, wout_hbm, dw1_hbm, dw2_hbm,
    res, rin, mesh, dw1, dw2,
    x, enc, feat, state, nall, hid, qt, sown, bias, wvo, sel,
    ew1, ew2, wqkv, wout, gain, gw, mw, gwt, mwt,
    psend, precv, wy, asend, arecv, xrecv, gown, mown, neigh, *rest,
):
    nc = CHUNKS
    cands = rest[:nc]
    lsem, ssem, r1, r1x, r2, r2x, r3, rx, ready = rest[nc:]
    nb, rows, depth = x.shape
    heads = depth // HD
    r = rows // nc
    m = nb * r
    count = lax.axis_size("tile") * lax.axis_size("sub")
    me = lax.axis_index("tile") * lax.axis_size("sub") + lax.axis_index("sub")

    def place(delta):
        d = lax.rem(me + delta + count, count)
        return (d // 2, lax.rem(d, 2))

    def offset(block):
        return lax.rem(block - me + 2 + count, count)

    place_in_plane = lax.rem(me, PLANE)
    inner = jnp.logical_and(place_in_plane > 1, place_in_plane < PLANE - 2)
    first_plane = me < PLANE
    last_plane = me >= count - PLANE

    def tell(sem, delta):
        pl.semaphore_signal(
            sem, inc=1, device_id=place(delta), device_id_type=pl.DeviceIdType.MESH
        )

    barrier = pltpu.get_barrier_semaphore()
    for delta in DELTAS:
        @pl.when(jnp.logical_not(crosses_up(place_in_plane, delta)))
        def _(delta=delta):
            tell(barrier, delta)

    def enter(cross):
        right = bool(cross) and cross[0] < 0
        pl.semaphore_wait(barrier, len(DELTAS) - (len(cross) if right else 0))
        if cross and not right:
            for delta in cross:
                tell(ready, delta)

    loads = {}

    def load(name, src, dst):
        c = pltpu.make_async_copy(src, dst, lsem.at[len(loads)])
        c.start()
        loads[name] = c

    load("gown", gown_hbm, gown)
    load("gw", gw_hbm, gw)
    load("mown", mown_hbm, mown)
    load("mw", mw_hbm, mw)
    load("neigh", neigh_hbm, neigh)
    load("gain", gain_hbm, gain)
    load("x0", grid_hbm.at[:, 0:r, :], x.at[:, 0:r, :])
    width = 512
    ff = ew1.shape[1]
    for f in range(0, ff, width):
        load(f"ew1_{f}", ew1_hbm.at[:, f:f + width], ew1.at[:, f:f + width])
    load("ew2", ew2_hbm, ew2)
    for c in range(1, nc):
        load(f"x{c}", grid_hbm.at[:, c * r:(c + 1) * r, :], x.at[:, c * r:(c + 1) * r, :])
    load("feat", feat_hbm, feat)
    load("wqkv", wqkv_hbm.at[0], wqkv)
    load("wout", wout_hbm.at[0], wout)
    load("dw1", dw1_hbm, dw1)
    load("dw2", dw2_hbm, dw2)

    for name in ("gown", "gw", "mown", "mw", "neigh"):
        loads[name].wait()
    gwt[...] = jnp.tile(gw[...], (rows // nb, 1)).T
    mwt[...] = jnp.tile(mw[...], (rows // nb, 1)).T

    out_row = lax.broadcasted_iota(jnp.int32, (r, r), 0)
    in_row = lax.broadcasted_iota(jnp.int32, (r, r), 1)
    same = (out_row == in_row).astype(F32)
    for b in range(nb):
        e = offset(gown[b])
        for s in range(5):
            hit = jnp.where(e == s, 1.0, 0.0).astype(F32)
            sel[s * r:(s + 1) * r, b * r:(b + 1) * r] = (same * hit).astype(BF)
    for delta, s in SLOT.items():
        listed = jnp.int32(0)
        for j in range(3):
            listed = listed + jnp.where(offset(neigh[0, j]) == 2 + delta, 1, 0)
        fill = jnp.where(listed > 0, 0.0, NEG).astype(F32)
        bias[:, s * rows:(s + 1) * rows] = jnp.full((1, rows), fill, F32)

    def remote(src, dst, ssem, rsem, delta):
        return pltpu.make_async_remote_copy(
            src_ref=src, dst_ref=dst, send_sem=ssem, recv_sem=rsem,
            device_id=place(delta), device_id_type=pl.DeviceIdType.MESH,
        )

    def spot(c):
        return slice(c * r, (c + 1) * r)

    def first(c, delta, cross=()):
        k = SLOT[delta]
        return remote(
            psend.at[c, k], precv.at[c, k], ssem.at[0],
            (r1x if delta in cross else r1).at[c], delta,
        )

    def second(c, delta):
        return remote(
            nall.at[OWN, spot(c), :], nall.at[SLOT[-delta], spot(c), :],
            ssem.at[1], r2.at[0], delta,
        )

    def across(c, delta):
        return remote(asend.at[c], arecv.at[c, SLOT[delta]], ssem.at[1], r2x.at[0], delta)

    def shared(c, partner, target):
        return remote(psend.at[c, SLOT[target]], xrecv.at[c], ssem.at[2], rx.at[0], partner)

    def third(c, delta):
        cand = cands[c]
        return remote(cand.at[2], cand.at[2 - delta], ssem.at[3], r3.at[c], delta)

    def arrived(ref, sem):
        remote(ref, ref, ssem.at[0], sem, 1).wait_recv()

    def left(ref, sem):
        remote(ref, ref, sem, r1.at[0], 1).wait_send()

    def local(cross):
        return [d for d in DELTAS if d not in cross]

    def norm(total):
        mean_sq = jnp.mean(total * total, axis=-1, keepdims=True)
        return (total * lax.rsqrt(mean_sq + 1e-06) * gain[...]).astype(BF)

    def add(c, sources):
        total = state[spot(c), :]
        for source in sources:
            total = total + precv[c, SLOT[-source]].astype(F32)
        state[spot(c), :] = total
        return total

    def finish(c, sources, targets, sem):
        arrived(precv.at[c, 0:len(sources)], sem.at[c])
        total = add(c, sources)
        nall[OWN, spot(c), :] = norm(total)
        for delta in targets:
            second(c, delta).start()

    def presum(c, cross):
        here = local(cross)
        arrived(precv.at[c, 0:len(here)], r1.at[c])
        asend[c] = add(c, here).astype(BF)
        for delta in cross:
            across(c, delta).start()

    def open_right(done, cross):
        pl.semaphore_wait(ready, len(cross))
        for c in range(done):
            for delta in cross:
                first(c, delta, cross).start()

    def absorb(c, late=False):
        @pl.when(inner)
        def _():
            finish(c, DELTAS, DELTAS, r1)

        for q, cross, _, _ in EDGES:
            right = cross[0] < 0
            on = place_in_plane == q
            if right and not late:
                on = jnp.logical_and(on, jnp.logical_not(first_plane))

            @pl.when(on)
            def _(cross=cross):
                presum(c, cross)

    def contribute(c):
        part = dot(sel[...], wy[...])
        if c == 0:
            loads["feat"].wait()
            loads["gain"].wait()
        state[spot(c), :] = feat[spot(c), :].astype(F32) + part[2 * r:3 * r]
        for delta in DELTAS:
            psend[c, SLOT[delta]] = part[(2 + delta) * r:(3 + delta) * r].astype(BF)

        @pl.when(inner)
        def _():
            if c == 0:
                enter(())
            for delta in DELTAS:
                first(c, delta).start()

        for q, cross, partner, target in EDGES:
            right = cross[0] < 0

            @pl.when(place_in_plane == q)
            def _(cross=cross, partner=partner, target=target, right=right):
                if c == 0:
                    if right:
                        enter(cross)
                    else:
                        pl.when(jnp.logical_not(last_plane))(lambda: enter(cross))
                if not right:
                    for delta in cross:
                        first(c, delta, cross).start()
                elif c >= LAG:
                    @pl.when(jnp.logical_not(first_plane))
                    def _():
                        for delta in cross:
                            first(c, delta, cross).start()
                for delta in local(cross):
                    first(c, delta, cross).start()
                shared(c, partner, target).start()

    for q, cross, _, _ in EDGES:
        if cross[0] > 0:
            @pl.when(jnp.logical_and(place_in_plane == q, last_plane))
            def _(cross=cross):
                enter(cross)

    for c in range(nc):
        loads[f"x{c}"].wait()
        xb = x[:, spot(c), :].reshape(m, depth)
        hidden_layer(xb, ew1, hid, lambda f, c=c: c == 0 and loads[f"ew1_{f}"].wait())
        if c > 0:
            contribute(c - 1)
        if c == 0:
            loads["ew2"].wait()
        wcol = jnp.concatenate([gwt[spot(c), b:b + 1] for b in range(nb)], axis=0)
        y = xb.astype(F32) + dot(hid[...], ew2[...])
        enc[:, spot(c), :] = y.astype(BF).reshape(nb, r, depth)
        wy[...] = (y * wcol).astype(BF)
        if c == LAG:
            for q, cross, _, _ in EDGES:
                if cross[0] < 0:
                    @pl.when(jnp.logical_and(place_in_plane == q, jnp.logical_not(first_plane)))
                    def _(cross=cross):
                        open_right(LAG, cross)
        if c == nc - 1:
            contribute(c)
        if c >= LAG:
            absorb(c - LAG)
    for q, cross, _, _ in EDGES:
        if cross[0] < 0:
            @pl.when(jnp.logical_and(place_in_plane == q, first_plane))
            def _(cross=cross):
                open_right(nc, cross)
                for c in range(nc - LAG):
                    presum(c, cross)
    for c in range(nc - LAG, nc - 1):
        absorb(c, True)

    loads["wqkv"].wait()
    loads["wout"].wait()
    for h in range(heads):
        cols = slice(2 * depth + h * HD, 2 * depth + (h + 1) * HD)
        wvo[h * depth:(h + 1) * depth, :] = dot(
            wqkv[:, cols], wout[h * HD:(h + 1) * HD, :]
        ).astype(BF)
    absorb(nc - 1, True)
    for q, cross, _, _ in EDGES:
        @pl.when(place_in_plane == q)
        def _(cross=cross):
            for c in range(nc):
                finish(c, cross, local(cross), r1x)

    parts = 2
    ar = rows // parts
    scale = HD ** -0.5
    q = dot(nall[OWN], wqkv[:, :depth]).astype(BF)
    for h in range(heads):
        t = scale * dot_nt(
            q[:, h * HD:(h + 1) * HD], wqkv[:, depth + h * HD:depth + (h + 1) * HD]
        )
        for p in range(parts):
            qt[p, h * ar:(h + 1) * ar, :] = t[p * ar:(p + 1) * ar].astype(BF)
    for p in range(parts):
        sown[p] = dot_nt(qt[p], nall[OWN])

    @pl.when(inner)
    def _():
        arrived(nall.at[0:OWN], r2.at[0])

    for q, cross, partner, target in EDGES:
        @pl.when(place_in_plane == q)
        def _(cross=cross, target=target):
            arrived(nall.at[0:OWN - len(cross)], r2.at[0])
            arrived(xrecv, rx.at[0])
            arrived(arecv.at[:, 0:len(cross)], r2x.at[0])
            for c in range(nc):
                for source in cross:
                    total = arecv[c, SLOT[-source]].astype(F32)
                    total = total + psend[c, SLOT[source]].astype(F32)
                    if source == target:
                        total = total + xrecv[c].astype(F32)
                    nall[SLOT[source], spot(c), :] = norm(total)

    per = nc // parts
    for p in range(parts):
        scores = dot_nt(qt[p], nall[0:OWN].reshape(OWN * rows, depth)) + bias[...]
        scores = jnp.concatenate([scores, sown[p]], axis=1)
        top = jnp.max(scores, axis=-1, keepdims=True)
        e = jnp.exp(scores - top)
        total = jnp.sum(e, axis=-1, keepdims=True)
        mixed = dot(e.astype(BF), nall[...].reshape(5 * rows, depth))
        mixed = (mixed / total).astype(BF)
        mixed = jnp.concatenate([mixed[h * ar:(h + 1) * ar] for h in range(heads)], axis=1)
        new = (state[p * ar:(p + 1) * ar, :] + dot(mixed, wvo[...])).astype(BF)
        mesh[p * ar:(p + 1) * ar, :] = new
        for i in range(per):
            c = p * per + i
            cands[c][2] = new[i * r:(i + 1) * r]
            for delta in DELTAS:
                third(c, delta).start()

    loads["dw1"].wait()
    loads["dw2"].wait()
    for c in range(nc):
        lo, hi = c * r, (c + 1) * r
        arrived(psend.at[c], r3.at[c])
        pieces = []
        for b in range(nb):
            e = jnp.minimum(offset(mown[b]), 4)
            pieces.append(
                enc[b, lo:hi, :].astype(F32)
                + mwt[lo:hi, b:b + 1] * cands[c][e].astype(F32)
            )
        rows_in = jnp.concatenate(pieces, axis=0).astype(BF)
        if c == nc - 1:
            rin[...] = rows_in
            break
        hidden_layer(rows_in, dw1, hid)
        y = rows_in.astype(F32) + dot(hid[...], dw2[...])
        res[:, lo:hi, :] = y.astype(BF).reshape(nb, r, depth)
    for i in (0, 1, 3):
        left(psend, ssem.at[i])

    @pl.when(jnp.logical_not(inner))
    def _():
        left(xrecv, ssem.at[2])


def last_kernel(res, rin, mesh, dw1, dw2, dec_hbm, mesh_hbm, hid, tail, sem):
    nb, rows, depth = res.shape
    m = rin.shape[0]
    r = m // nb
    done = rows - r
    outs = [
        pltpu.make_async_copy(
            res.at[:, 0:done, :], dec_hbm.at[:, 0:done, :], sem.at[0]
        ),
        pltpu.make_async_copy(mesh, mesh_hbm, sem.at[1]),
    ]
    for out in outs:
        out.start()
    rows_in = rin[...]
    hidden_layer(rows_in, dw1, hid)
    y = rows_in.astype(F32) + dot(hid[...], dw2[...])
    tail[...] = y.astype(BF).reshape(nb, r, depth)
    out = pltpu.make_async_copy(tail, dec_hbm.at[:, done:, :], sem.at[2])
    out.start()
    outs.append(out)
    for out in outs:
        out.wait()


def on_device(
    grid, g2m_owner, g2m_weight, m2g_owner, m2g_weight, mesh_feat, neighbours,
    enc_w1, enc_w2, attn_gain, w_qkv, w_out, dec_w1, dec_w2,
):
    nb = g2m_owner.shape[0]
    rows, depth = mesh_feat.shape
    ff = enc_w1.shape[1]
    nc = CHUNKS
    r = rows // nc
    nd = len(DELTAS)
    heads = depth // HD
    any_spec = pl.BlockSpec(memory_space=pl.ANY)
    vm_spec = pl.BlockSpec(memory_space=pltpu.VMEM)
    dma = pltpu.SemaphoreType.DMA
    vm = pltpu.VMEM
    held = pl.pallas_call(
        step_kernel,
        out_shape=(
            vm((nb, rows, depth), BF),
            vm((nb * r, depth), BF),
            vm((rows, depth), BF),
            vm((depth, ff), BF),
            vm((ff, depth), BF),
        ),
        in_specs=[pl.BlockSpec(memory_space=pltpu.HBM)] * 14,
        out_specs=(vm_spec,) * 5,
        scratch_shapes=[
            vm((nb, rows, depth), BF),
            vm((nb, rows, depth), BF),
            vm((rows, depth), BF),
            vm((rows, depth), F32),
            vm((5, rows, depth), BF),
            vm((nb * r, ff), BF),
            vm((2, rows // 2 * heads, depth), BF),
            vm((2, rows // 2 * heads, rows), F32),
            vm((1, OWN * rows), F32),
            vm((heads * depth, depth), BF),
            vm((5 * r, nb * r), BF),
            vm((depth, ff), BF),
            vm((ff, depth), BF),
            vm((depth, 3 * depth), BF),
            vm((depth, depth), BF),
            vm((1, depth), F32),
            vm((nb, rows), F32),
            vm((nb, rows), F32),
            vm((rows, rows), F32),
            vm((rows, rows), F32),
            vm((nc, nd, r, depth), BF),
            vm((nc, nd, r, depth), BF),
            vm((nb * r, depth), BF),
            vm((nc, r, depth), BF),
            vm((nc, nd, r, depth), BF),
            vm((nc, r, depth), BF),
            pltpu.SMEM((nb,), jnp.int32),
            pltpu.SMEM((nb,), jnp.int32),
            pltpu.SMEM((1, 3), jnp.int32),
        ]
        + [vm((5, r, depth), BF)] * nc
        + [dma((22,))]
        + [dma((4,)), dma((nc,)), dma((nc,)), dma((1,)), dma((1,)), dma((nc,)), dma((1,))]
        + [pltpu.SemaphoreType.REGULAR],
        compiler_params=pltpu.CompilerParams(
            collective_id=0, has_side_effects=True, vmem_limit_bytes=40 * 2**20
        ),
        name="step",
    )(*[pltpu.with_memory_space_constraint(a, pltpu.HBM) for a in (
        grid.reshape(nb, rows, depth), g2m_owner, g2m_weight.reshape(nb, rows),
        m2g_owner, m2g_weight.reshape(nb, rows), mesh_feat, neighbours,
        enc_w1, enc_w2, attn_gain, w_qkv, w_out, dec_w1, dec_w2,
    )])
    decoded, mesh_out = pl.pallas_call(
        last_kernel,
        out_shape=(
            jax.ShapeDtypeStruct((nb, rows, depth), BF),
            jax.ShapeDtypeStruct((rows, depth), BF),
        ),
        in_specs=[vm_spec] * 5,
        out_specs=(any_spec, any_spec),
        scratch_shapes=[
            vm((nb * r, ff), BF),
            vm((nb, r, depth), BF),
            dma((3,)),
        ],
        compiler_params=pltpu.CompilerParams(vmem_limit_bytes=16 * 2**20),
        name="last",
    )(*[pltpu.with_memory_space_constraint(a, pltpu.VMEM) for a in held])
    return decoded.reshape(nb * rows, depth), mesh_out


def solution(mesh):
    cut = P(("tile", "sub"))
    cut2 = P(("tile", "sub"), None)
    in_specs = (cut2, cut, cut, cut, cut, cut2, cut2) + (P(),) * 7
    return jax.shard_map(
        on_device, mesh=mesh, in_specs=in_specs, out_specs=(cut2, cut2), check_vma=False
    )
```

```python
import functools

import jax
import jax.numpy as jnp
from jax import lax
from jax.experimental import pallas as pl
from jax.experimental.pallas import tpu as pltpu
from jax.sharding import PartitionSpec as P

HD = 128
DELTAS = (-2, 2, -1, 1)
SLOT = {-2: 0, -1: 1, 1: 2, 2: 3}
OWN = 4
CHUNKS = 4
LAG = 3
NEG = -1e30
PLANE = 32
EDGES = (
    (0, (-2, -1), 1, -1),
    (1, (-2,), -1, -2),
    (PLANE - 2, (2,), 1, 2),
    (PLANE - 1, (1, 2), -1, 1),
)
BF = jnp.bfloat16
F32 = jnp.float32
NT = (((1,), (1,)), ((), ()))


def dot(a, b):
    return jnp.dot(a, b, preferred_element_type=F32)


def dot_nt(a, b):
    return lax.dot_general(a, b, NT, preferred_element_type=F32)


def crosses_up(position, delta):
    if delta < 0:
        return jnp.bool_(False)
    return jnp.logical_and(position < PLANE, position + delta >= PLANE)


def hidden_layer(rows, w1, hid, ready=lambda f: None):
    width = 512
    for f in range(0, w1.shape[1], width):
        ready(f)
        cols = slice(f, f + width)
        half = 0.5 * dot(rows, w1[:, cols])
        hid[:, cols] = (half + half * jnp.tanh(half)).astype(BF)


def step_kernel(
    grid_hbm, gown_hbm, gw_hbm, mown_hbm, mw_hbm, feat_hbm, neigh_hbm,
    ew1_hbm, ew2_hbm, gain_hbm, wqkv_hbm, wout_hbm, dw1_hbm, dw2_hbm,
    res, rin, mesh, hout, dw2,
    x, enc, feat, state, nall, hid, dw1, qt, sown, bias, wvo, sel,
    ew1, ew2, wqkv, wout, gain, gw, mw, gwt, mwt,
    psend, precv, csend, asend, arecv, xrecv, gown, mown, neigh, *rest,
):
    nc = CHUNKS
    cands = rest[:nc]
    lsem, ssem, r1, r1x, r2, r2x, r3, rx, ready = rest[nc:]
    nb, rows, depth = x.shape
    heads = depth // HD
    r = rows // nc
    m = nb * r
    count = lax.axis_size("tile") * lax.axis_size("sub")
    me = lax.axis_index("tile") * lax.axis_size("sub") + lax.axis_index("sub")

    def place(delta):
        d = lax.rem(me + delta + count, count)
        return (d // 2, lax.rem(d, 2))

    def offset(block):
        return lax.rem(block - me + 2 + count, count)

    place_in_plane = lax.rem(me, PLANE)
    inner = jnp.logical_and(place_in_plane > 1, place_in_plane < PLANE - 2)
    last_plane = me >= count - PLANE

    def tell(sem, delta):
        pl.semaphore_signal(
            sem, inc=1, device_id=place(delta), device_id_type=pl.DeviceIdType.MESH
        )

    barrier = pltpu.get_barrier_semaphore()
    for delta in DELTAS:
        @pl.when(jnp.logical_not(crosses_up(place_in_plane, delta)))
        def _(delta=delta):
            tell(barrier, delta)

    def enter(cross):
        right = bool(cross) and cross[0] < 0
        pl.semaphore_wait(barrier, len(DELTAS) - (len(cross) if right else 0))
        if cross and not right:
            for delta in cross:
                tell(ready, delta)

    loads = {}

    def load(name, src, dst):
        c = pltpu.make_async_copy(src, dst, lsem.at[len(loads)])
        c.start()
        loads[name] = c

    width = 512
    ff = ew1.shape[1]
    load("gown", gown_hbm, gown)
    load("gw", gw_hbm, gw)
    load("mown", mown_hbm, mown)
    load("mw", mw_hbm, mw)
    load("neigh", neigh_hbm, neigh)
    load("gain", gain_hbm, gain)
    load("x0", grid_hbm.at[:, 0:r, :], x.at[:, 0:r, :])
    for f in range(0, ff, width):
        load(f"ew1_{f}", ew1_hbm.at[:, f:f + width], ew1.at[:, f:f + width])
    load("ew2", ew2_hbm, ew2)
    for c in range(1, nc):
        load(
            f"x{c}", grid_hbm.at[:, c * r:(c + 1) * r, :], x.at[:, c * r:(c + 1) * r, :]
        )
    load("feat", feat_hbm, feat)
    load("wqkv", wqkv_hbm.at[0], wqkv)
    load("wout", wout_hbm.at[0], wout)
    load("dw1", dw1_hbm, dw1)
    load("dw2", dw2_hbm, dw2)

    for q, cross, _, _ in EDGES:
        if cross[0] > 0:
            @pl.when(jnp.logical_and(place_in_plane == q, last_plane))
            def _(cross=cross):
                enter(cross)

    for name in ("gown", "gw", "mown", "mw", "neigh"):
        loads[name].wait()
    gwt[...] = jnp.tile(gw[...], (rows // nb, 1)).T
    mwt[...] = jnp.tile(mw[...], (rows // nb, 1)).T

    out_row = lax.broadcasted_iota(jnp.int32, (r, r), 0)
    in_row = lax.broadcasted_iota(jnp.int32, (r, r), 1)
    same = (out_row == in_row).astype(F32)
    for b in range(nb):
        e = offset(gown[b])
        for s in range(5):
            hit = jnp.where(e == s, 1.0, 0.0).astype(F32)
            sel[s * r:(s + 1) * r, b * r:(b + 1) * r] = (same * hit).astype(BF)
    for delta, s in SLOT.items():
        listed = jnp.int32(0)
        for j in range(3):
            listed = listed + jnp.where(offset(neigh[0, j]) == 2 + delta, 1, 0)
        fill = jnp.where(listed > 0, 0.0, NEG).astype(F32)
        bias[:, s * rows:(s + 1) * rows] = jnp.full((1, rows), fill, F32)

    def remote(src, dst, ssem, rsem, delta):
        return pltpu.make_async_remote_copy(
            src_ref=src, dst_ref=dst, send_sem=ssem, recv_sem=rsem,
            device_id=place(delta), device_id_type=pl.DeviceIdType.MESH,
        )

    def spot(c):
        return slice(c * r, (c + 1) * r)

    def first(c, delta, cross=()):
        k = SLOT[delta]
        return remote(
            psend.at[c, k], precv.at[c, k], ssem.at[0],
            (r1x if delta in cross else r1).at[c], delta,
        )

    def second(c, delta):
        return remote(
            nall.at[OWN, spot(c), :], nall.at[SLOT[-delta], spot(c), :],
            ssem.at[1], r2.at[0], delta,
        )

    def across(c, delta):
        return remote(asend.at[c], arecv.at[c, SLOT[delta]], ssem.at[1], r2x.at[0], delta)

    def shared(c, partner, target):
        return remote(psend.at[c, SLOT[target]], xrecv.at[c], ssem.at[2], rx.at[c], partner)

    def both(c, target):
        k = SLOT[target]
        return remote(csend.at[c], precv.at[c, k], ssem.at[0], r1x.at[c], target)

    def cross_over(c, partner, target):
        if abs(target) == 2:
            arrived(xrecv.at[c], rx.at[c])
            csend[c] = (
                psend[c, SLOT[target]].astype(F32) + xrecv[c].astype(F32)
            ).astype(BF)
            both(c, target).start()
        else:
            first(c, 2 * target, (2 * target,)).start()

    def third(c, delta):
        cand = cands[c]
        return remote(cand.at[2], cand.at[2 - delta], ssem.at[3], r3.at[c], delta)

    def arrived(ref, sem):
        remote(ref, ref, ssem.at[0], sem, 1).wait_recv()

    def left(ref, sem):
        remote(ref, ref, sem, r1.at[0], 1).wait_send()

    def far(cross):
        return -2 if cross[0] < 0 else 2

    def local(cross):
        return [d for d in DELTAS if d not in cross]

    def norm(total):
        mean_sq = jnp.mean(total * total, axis=-1, keepdims=True)
        return (total * lax.rsqrt(mean_sq + 1e-06) * gain[...]).astype(BF)

    def add(c, sources):
        total = state[spot(c), :]
        for source in sources:
            total = total + precv[c, SLOT[-source]].astype(F32)
        state[spot(c), :] = total
        return total

    def finish(c, sources, targets, sem):
        arrived(precv.at[c, 0:len(sources)], sem.at[c])
        total = add(c, sources)
        nall[OWN, spot(c), :] = norm(total)
        for delta in targets:
            second(c, delta).start()

    def presum(c, cross):
        here = local(cross)
        arrived(precv.at[c, 0:len(here)], r1.at[c])
        asend[c] = add(c, here).astype(BF)
        for delta in cross:
            across(c, delta).start()

    def open_right(done, cross, partner, target):
        pl.semaphore_wait(ready, len(cross))
        for c in range(done):
            cross_over(c, partner, target)

    def absorb(c, late=False):
        @pl.when(inner)
        def _():
            finish(c, DELTAS, DELTAS, r1)

        if late:
            for q, cross, _, _ in EDGES:
                @pl.when(place_in_plane == q)
                def _(cross=cross):
                    presum(c, cross)

    def contribute(c, part):
        state[spot(c), :] = feat[spot(c), :].astype(F32) + part[2 * r:3 * r]
        for delta in DELTAS:
            psend[c, SLOT[delta]] = part[(2 + delta) * r:(3 + delta) * r].astype(BF)

        @pl.when(inner)
        def _():
            if c == 0:
                enter(())
            for delta in DELTAS:
                first(c, delta).start()

        for q, cross, partner, target in EDGES:
            right = cross[0] < 0

            @pl.when(place_in_plane == q)
            def _(cross=cross, partner=partner, target=target, right=right):
                if c == 0 and right:
                    enter(cross)
                for delta in local(cross):
                    first(c, delta, cross).start()
                shared(c, partner, target).start()
                if not right and 0 < c:
                    cross_over(c - 1, partner, target)

    def open_chunk(c, ready=lambda f: None):
        hidden_layer(x[:, spot(c), :].reshape(m, depth), ew1, hid.at[c % 2], ready)

    loads["x0"].wait()
    open_chunk(0, lambda f: loads[f"ew1_{f}"].wait())
    for q, cross, _, _ in EDGES:
        if cross[0] > 0:
            @pl.when(jnp.logical_and(place_in_plane == q, jnp.logical_not(last_plane)))
            def _(cross=cross):
                enter(cross)

    for name in ["ew2", "feat", "gain"] + [f"x{c}" for c in range(1, nc)]:
        loads[name].wait()
    for c in range(nc):
        for _ in range(1):
            wcol = jnp.concatenate([gwt[spot(c), b:b + 1] for b in range(nb)], axis=0)
            y = x[:, spot(c), :].reshape(m, depth).astype(F32) + dot(hid[c % 2], ew2[...])
            enc[:, spot(c), :] = y.astype(BF).reshape(nb, r, depth)
            wy = (y * wcol).astype(BF)
            if c < nc - 1:
                open_chunk(c + 1)
            part = dot(sel[...], wy)
        contribute(c, part)
        if c >= LAG:
            absorb(c - LAG)
    for q, cross, partner, target in EDGES:
        right = cross[0] < 0

        @pl.when(place_in_plane == q)
        def _(cross=cross, partner=partner, target=target, right=right):
            if right:
                open_right(nc, cross, partner, target)
            else:
                cross_over(nc - 1, partner, target)
            for c in range(nc - LAG):
                presum(c, cross)

    for c in range(nc - LAG, nc - 1):
        absorb(c, True)

    loads["wqkv"].wait()
    loads["wout"].wait()
    for h in range(heads):
        cols = slice(2 * depth + h * HD, 2 * depth + (h + 1) * HD)
        wvo[h * depth:(h + 1) * depth, :] = dot(
            wqkv[:, cols], wout[h * HD:(h + 1) * HD, :]
        ).astype(BF)
    absorb(nc - 1, True)
    for q, cross, _, _ in EDGES:
        @pl.when(place_in_plane == q)
        def _(cross=cross):
            for c in range(nc):
                finish(c, (far(cross),), local(cross), r1x)

    parts = 2
    ar = rows // parts
    scale = HD ** -0.5
    q = dot(nall[OWN], wqkv[:, :depth]).astype(BF)
    for h in range(heads):
        t = scale * dot_nt(
            q[:, h * HD:(h + 1) * HD], wqkv[:, depth + h * HD:depth + (h + 1) * HD]
        )
        for p in range(parts):
            qt[p, h * ar:(h + 1) * ar, :] = t[p * ar:(p + 1) * ar].astype(BF)
    for p in range(parts):
        sown[p] = dot_nt(qt[p], nall[OWN])

    @pl.when(inner)
    def _():
        arrived(nall.at[0:OWN], r2.at[0])

    for q, cross, partner, target in EDGES:
        @pl.when(place_in_plane == q)
        def _(cross=cross, target=target):
            arrived(nall.at[0:OWN - len(cross)], r2.at[0])
            if abs(target) == 1:
                for c in range(nc):
                    arrived(xrecv.at[c], rx.at[c])
            arrived(arecv.at[:, 0:len(cross)], r2x.at[0])
            for c in range(nc):
                for source in cross:
                    total = arecv[c, SLOT[-source]].astype(F32)
                    total = total + psend[c, SLOT[source]].astype(F32)
                    if source == target:
                        total = total + xrecv[c].astype(F32)
                    nall[SLOT[source], spot(c), :] = norm(total)

    per = nc // parts
    for p in range(parts):
        scores = dot_nt(qt[p], nall[0:OWN].reshape(OWN * rows, depth)) + bias[...]
        scores = jnp.concatenate([scores, sown[p]], axis=1)
        top = jnp.max(scores, axis=-1, keepdims=True)
        e = jnp.exp(scores - top)
        total = jnp.sum(e, axis=-1, keepdims=True)
        mixed = dot(e.astype(BF), nall[...].reshape(5 * rows, depth))
        mixed = (mixed / total).astype(BF)
        mixed = jnp.concatenate([mixed[h * ar:(h + 1) * ar] for h in range(heads)], axis=1)
        new = (state[p * ar:(p + 1) * ar, :] + dot(mixed, wvo[...])).astype(BF)
        mesh[p * ar:(p + 1) * ar, :] = new
        for i in range(per):
            c = p * per + i
            cands[c][2] = new[i * r:(i + 1) * r]
            for delta in DELTAS:
                third(c, delta).start()

    loads["dw1"].wait()
    loads["dw2"].wait()
    def read(c):
        arrived(psend.at[c], r3.at[c])
        pieces = []
        for b in range(nb):
            e = jnp.minimum(offset(mown[b]), 4)
            pieces.append(
                enc[b, spot(c), :].astype(F32)
                + mwt[spot(c), b:b + 1] * cands[c][e].astype(F32)
            )
        return jnp.concatenate(pieces, axis=0).astype(BF)

    rows_in = read(0)
    hidden_layer(rows_in, dw1, hid.at[0])
    for c in range(nc - 1):
        after = read(c + 1)
        for _ in range(1):
            y = rows_in.astype(F32) + dot(hid[c % 2], dw2[...])
            res[:, spot(c), :] = y.astype(BF).reshape(nb, r, depth)
            hidden_layer(after, dw1, hout if c == nc - 2 else hid.at[(c + 1) % 2])
        rows_in = after
    rin[...] = rows_in
    for i in (1, 3):
        left(psend, ssem.at[i])

    @pl.when(inner)
    def _():
        left(psend, ssem.at[0])

    for q, cross, _, _ in EDGES:
        @pl.when(place_in_plane == q)
        def _(cross=cross):
            left(psend.at[:, 0:len(local(cross)) + 1], ssem.at[0])
            left(xrecv, ssem.at[2])


def last_kernel(res, rin, mesh, hid, dw2, dec_hbm, mesh_hbm, tail, sem):
    nb, rows, depth = res.shape
    m = rin.shape[0]
    r = m // nb
    done = rows - r
    outs = [
        pltpu.make_async_copy(
            res.at[:, 0:done, :], dec_hbm.at[:, 0:done, :], sem.at[0]
        ),
        pltpu.make_async_copy(mesh, mesh_hbm, sem.at[1]),
    ]
    for out in outs:
        out.start()
    y = rin[...].astype(F32) + dot(hid[...], dw2[...])
    tail[...] = y.astype(BF).reshape(nb, r, depth)
    out = pltpu.make_async_copy(tail, dec_hbm.at[:, done:, :], sem.at[2])
    out.start()
    outs.append(out)
    for out in outs:
        out.wait()


def on_device(
    grid, g2m_owner, g2m_weight, m2g_owner, m2g_weight, mesh_feat, neighbours,
    enc_w1, enc_w2, attn_gain, w_qkv, w_out, dec_w1, dec_w2,
):
    nb = g2m_owner.shape[0]
    rows, depth = mesh_feat.shape
    ff = enc_w1.shape[1]
    nc = CHUNKS
    r = rows // nc
    nd = len(DELTAS)
    heads = depth // HD
    any_spec = pl.BlockSpec(memory_space=pl.ANY)
    vm_spec = pl.BlockSpec(memory_space=pltpu.VMEM)
    dma = pltpu.SemaphoreType.DMA
    vm = pltpu.VMEM
    held = pl.pallas_call(
        step_kernel,
        out_shape=(
            vm((nb, rows, depth), BF),
            vm((nb * r, depth), BF),
            vm((rows, depth), BF),
            vm((nb * r, ff), BF),
            vm((ff, depth), BF),
        ),
        in_specs=[pl.BlockSpec(memory_space=pltpu.HBM)] * 14,
        out_specs=(vm_spec,) * 5,
        scratch_shapes=[
            vm((nb, rows, depth), BF),
            vm((nb, rows, depth), BF),
            vm((rows, depth), BF),
            vm((rows, depth), F32),
            vm((5, rows, depth), BF),
            vm((2, nb * r, ff), BF),
            vm((depth, ff), BF),
            vm((2, rows // 2 * heads, depth), BF),
            vm((2, rows // 2 * heads, rows), F32),
            vm((1, OWN * rows), F32),
            vm((heads * depth, depth), BF),
            vm((5 * r, nb * r), BF),
            vm((depth, ff), BF),
            vm((ff, depth), BF),
            vm((depth, 3 * depth), BF),
            vm((depth, depth), BF),
            vm((1, depth), F32),
            vm((nb, rows), F32),
            vm((nb, rows), F32),
            vm((rows, rows), F32),
            vm((rows, rows), F32),
            vm((nc, nd, r, depth), BF),
            vm((nc, nd, r, depth), BF),
            vm((nc, r, depth), BF),
            vm((nc, r, depth), BF),
            vm((nc, nd, r, depth), BF),
            vm((nc, r, depth), BF),
            pltpu.SMEM((nb,), jnp.int32),
            pltpu.SMEM((nb,), jnp.int32),
            pltpu.SMEM((1, 3), jnp.int32),
        ]
        + [vm((5, r, depth), BF)] * nc
        + [dma((22,))]
        + [dma((4,)), dma((nc,)), dma((nc,)), dma((1,)), dma((1,)), dma((nc,)), dma((nc,))]
        + [pltpu.SemaphoreType.REGULAR],
        compiler_params=pltpu.CompilerParams(
            collective_id=0, has_side_effects=True, vmem_limit_bytes=40 * 2**20
        ),
        name="step",
    )(*[pltpu.with_memory_space_constraint(a, pltpu.HBM) for a in (
        grid.reshape(nb, rows, depth), g2m_owner, g2m_weight.reshape(nb, rows),
        m2g_owner, m2g_weight.reshape(nb, rows), mesh_feat, neighbours,
        enc_w1, enc_w2, attn_gain, w_qkv, w_out, dec_w1, dec_w2,
    )])
    decoded, mesh_out = pl.pallas_call(
        last_kernel,
        out_shape=(
            jax.ShapeDtypeStruct((nb, rows, depth), BF),
            jax.ShapeDtypeStruct((rows, depth), BF),
        ),
        in_specs=[vm_spec] * 5,
        out_specs=(any_spec, any_spec),
        scratch_shapes=[
            vm((nb, r, depth), BF),
            dma((3,)),
        ],
        compiler_params=pltpu.CompilerParams(vmem_limit_bytes=16 * 2**20),
        name="last",
    )(*[pltpu.with_memory_space_constraint(a, pltpu.VMEM) for a in held])
    return decoded.reshape(nb * rows, depth), mesh_out


def solution(mesh):
    cut = P(("tile", "sub"))
    cut2 = P(("tile", "sub"), None)
    in_specs = (cut2, cut, cut, cut, cut, cut2, cut2) + (P(),) * 7
    return jax.shard_map(
        on_device, mesh=mesh, in_specs=in_specs, out_specs=(cut2, cut2), check_vma=False
    )
```

```python
import functools

import jax
import jax.numpy as jnp
from jax import lax
from jax.experimental import pallas as pl
from jax.experimental.pallas import tpu as pltpu
from jax.sharding import PartitionSpec as P

HD = 128
DELTAS = (-2, 2, -1, 1)
SLOT = {-2: 0, -1: 1, 1: 2, 2: 3}
OWN = 4
CHUNKS = 4
LAG = 3
NEG = -1e30
PLANE = 32
SUMS = {
    0: (-1, (-2,), None, -1),
    1: (-2, (-2,), -2, None),
    PLANE - 2: (2, (), None, 2),
    PLANE - 1: (2, (1, 2), 1, None),
}
EDGES = (
    (0, (-2, -1), 1, -1),
    (1, (-2,), -1, -2),
    (PLANE - 2, (2,), 1, 2),
    (PLANE - 1, (1, 2), -1, 1),
)
BF = jnp.bfloat16
F32 = jnp.float32
NT = (((1,), (1,)), ((), ()))


def dot(a, b):
    return jnp.dot(a, b, preferred_element_type=F32)


def dot_nt(a, b):
    return lax.dot_general(a, b, NT, preferred_element_type=F32)


def crosses_up(position, delta):
    if delta < 0:
        return jnp.bool_(False)
    return jnp.logical_and(position < PLANE, position + delta >= PLANE)


def hidden_layer(rows, w1, hid):
    width = 512
    for f in range(0, w1.shape[1], width):
        cols = slice(f, f + width)
        half = 0.5 * dot(rows, w1[:, cols])
        hid[:, cols] = (half + half * jnp.tanh(half)).astype(BF)


def step_kernel(
    grid_hbm, gown_hbm, gw_hbm, mown_hbm, mw_hbm, feat_hbm, neigh_hbm,
    ew1_hbm, ew2_hbm, gain_hbm, wqkv_hbm, wout_hbm, dw1_hbm, dw2_hbm,
    res, rin, mesh, hout, dw2,
    x, enc, feat, state, nall, hid, dw1, qt, sown, bias, wvo, sel,
    ew1, ew2, wqkv, wout, gain, gw, mw, gwt, mwt,
    psend, precv, csend, asend, arecv, xrecv, gown, mown, neigh, *rest,
):
    nc = CHUNKS
    cands = rest[:nc]
    lsem, ssem, r1, r1x, r2, r2x, r2f, r3, rx, ready = rest[nc:]
    nb, rows, depth = x.shape
    heads = depth // HD
    r = rows // nc
    m = nb * r
    count = lax.axis_size("tile") * lax.axis_size("sub")
    me = lax.axis_index("tile") * lax.axis_size("sub") + lax.axis_index("sub")

    def place(delta):
        d = lax.rem(me + delta + count, count)
        return (d // 2, lax.rem(d, 2))

    def offset(block):
        return lax.rem(block - me + 2 + count, count)

    place_in_plane = lax.rem(me, PLANE)
    inner = jnp.logical_and(place_in_plane > 1, place_in_plane < PLANE - 2)
    last_plane = me >= count - PLANE

    def tell(sem, delta):
        pl.semaphore_signal(
            sem, inc=1, device_id=place(delta), device_id_type=pl.DeviceIdType.MESH
        )

    barrier = pltpu.get_barrier_semaphore()
    for delta in DELTAS:
        @pl.when(jnp.logical_not(crosses_up(place_in_plane, delta)))
        def _(delta=delta):
            tell(barrier, delta)

    def enter(cross):
        right = bool(cross) and cross[0] < 0
        pl.semaphore_wait(barrier, len(DELTAS) - (len(cross) if right else 0))
        if cross and not right:
            for delta in cross:
                tell(ready, delta)

    loads = {}

    def load(name, src, dst):
        c = pltpu.make_async_copy(src, dst, lsem.at[len(loads)])
        c.start()
        loads[name] = c

    load("gown", gown_hbm, gown)
    load("gw", gw_hbm, gw)
    load("mown", mown_hbm, mown)
    load("mw", mw_hbm, mw)
    load("neigh", neigh_hbm, neigh)
    load("gain", gain_hbm, gain)
    load("x0", grid_hbm.at[:, 0:r, :], x.at[:, 0:r, :])
    for k in range(0, depth, HD):
        load(f"ew1_{k}", ew1_hbm.at[k:k + HD, :], ew1.at[k:k + HD, :])
    load("ew2", ew2_hbm, ew2)
    for c in range(1, nc):
        load(
            f"x{c}", grid_hbm.at[:, c * r:(c + 1) * r, :], x.at[:, c * r:(c + 1) * r, :]
        )
    load("feat", feat_hbm, feat)
    load("wqkv", wqkv_hbm.at[0], wqkv)
    load("wout", wout_hbm.at[0], wout)
    load("dw1", dw1_hbm, dw1)
    load("dw2", dw2_hbm, dw2)

    for q, cross, _, _ in EDGES:
        if cross[0] > 0:
            @pl.when(jnp.logical_and(place_in_plane == q, last_plane))
            def _(cross=cross):
                enter(cross)

    for name in ("gown", "gw", "mown", "mw", "neigh"):
        loads[name].wait()
    gwt[...] = jnp.tile(gw[...], (rows // nb, 1)).T
    mwt[...] = jnp.tile(mw[...], (rows // nb, 1)).T

    out_row = lax.broadcasted_iota(jnp.int32, (r, r), 0)
    in_row = lax.broadcasted_iota(jnp.int32, (r, r), 1)
    same = (out_row == in_row).astype(F32)
    for b in range(nb):
        e = offset(gown[b])
        for s in range(5):
            hit = jnp.where(e == s, 1.0, 0.0).astype(F32)
            sel[s * r:(s + 1) * r, b * r:(b + 1) * r] = (same * hit).astype(BF)
    for delta, s in SLOT.items():
        listed = jnp.int32(0)
        for j in range(3):
            listed = listed + jnp.where(offset(neigh[0, j]) == 2 + delta, 1, 0)
        fill = jnp.where(listed > 0, 0.0, NEG).astype(F32)
        bias[:, s * rows:(s + 1) * rows] = jnp.full((1, rows), fill, F32)

    def remote(src, dst, ssem, rsem, delta):
        return pltpu.make_async_remote_copy(
            src_ref=src, dst_ref=dst, send_sem=ssem, recv_sem=rsem,
            device_id=place(delta), device_id_type=pl.DeviceIdType.MESH,
        )

    def spot(c):
        return slice(c * r, (c + 1) * r)

    def first(c, delta, cross=()):
        k = SLOT[delta]
        return remote(
            psend.at[c, k], precv.at[c, k], ssem.at[0],
            (r1x if delta in cross else r1).at[c], delta,
        )

    def second(c, delta):
        return remote(
            nall.at[OWN, spot(c), :], nall.at[SLOT[-delta], spot(c), :],
            ssem.at[1], r2.at[0], delta,
        )

    def across(c, delta):
        return remote(asend.at[c], arecv.at[c, SLOT[delta]], ssem.at[1], r2x.at[0], delta)

    def passed(c, partner, source):
        own, other = SLOT[-source], SLOT[partner - source]
        return remote(arecv.at[c, own], arecv.at[c, other], ssem.at[2], r2f.at[0], partner)

    def shared(c, partner, target):
        return remote(psend.at[c, SLOT[target]], xrecv.at[c], ssem.at[2], rx.at[c], partner)

    def both(c, target):
        k = SLOT[target]
        return remote(csend.at[c], precv.at[c, k], ssem.at[0], r1x.at[c], target)

    def cross_over(c, partner, target):
        if abs(target) == 2:
            arrived(xrecv.at[c], rx.at[c])
            csend[c] = (
                psend[c, SLOT[target]].astype(F32) + xrecv[c].astype(F32)
            ).astype(BF)
            both(c, target).start()
        else:
            first(c, 2 * target, (2 * target,)).start()

    def third(c, delta):
        cand = cands[c]
        return remote(cand.at[2], cand.at[2 - delta], ssem.at[3], r3.at[c], delta)

    def arrived(ref, sem):
        remote(ref, ref, ssem.at[0], sem, 1).wait_recv()

    def left(ref, sem):
        remote(ref, ref, sem, r1.at[0], 1).wait_send()

    def far(cross):
        return -2 if cross[0] < 0 else 2

    def local(cross):
        return [d for d in DELTAS if d not in cross]

    def norm(total):
        mean_sq = jnp.mean(total * total, axis=-1, keepdims=True)
        return (total * lax.rsqrt(mean_sq + 1e-06) * gain[...]).astype(BF)

    def add(c, sources):
        total = state[spot(c), :]
        for source in sources:
            total = total + precv[c, SLOT[-source]].astype(F32)
        state[spot(c), :] = total
        return total

    def finish(c, sources, targets, sem):
        arrived(precv.at[c, 0:len(sources)], sem.at[c])
        total = add(c, sources)
        nall[OWN, spot(c), :] = norm(total)
        for delta in targets:
            second(c, delta).start()

    def presum(c, cross, q):
        here = local(cross)
        arrived(precv.at[c, 0:len(here)], r1.at[c])
        asend[c] = add(c, here).astype(BF)
        across(c, SUMS[q][0]).start()

    def open_right(done, cross, partner, target):
        pl.semaphore_wait(ready, len(cross))
        for c in range(done):
            cross_over(c, partner, target)

    def absorb(c, late=False):
        @pl.when(inner)
        def _():
            finish(c, DELTAS, DELTAS, r1)

        if late:
            for q, cross, _, _ in EDGES:
                @pl.when(place_in_plane == q)
                def _(cross=cross, q=q):
                    presum(c, cross, q)

    def contribute(c, part):
        state[spot(c), :] = feat[spot(c), :].astype(F32) + part[2 * r:3 * r]
        for delta in DELTAS:
            psend[c, SLOT[delta]] = part[(2 + delta) * r:(3 + delta) * r].astype(BF)

        @pl.when(inner)
        def _():
            if c == 0:
                enter(())
            for delta in DELTAS:
                first(c, delta).start()

        for q, cross, partner, target in EDGES:
            right = cross[0] < 0

            @pl.when(place_in_plane == q)
            def _(cross=cross, partner=partner, target=target, right=right):
                if c == 0 and right:
                    enter(cross)
                for delta in local(cross):
                    first(c, delta, cross).start()
                shared(c, partner, target).start()
                if not right and len(cross) == 2:
                    cross_over(c, partner, target)
                if not right and len(cross) == 1 and c > 0:
                    cross_over(c - 1, partner, target)

    def open_chunk(c):
        hidden_layer(x[:, spot(c), :].reshape(m, depth), ew1, hid.at[c % 2])

    loads["x0"].wait()
    for k in range(0, depth, HD):
        loads[f"ew1_{k}"].wait()
    open_chunk(0)
    for q, cross, _, _ in EDGES:
        if cross[0] > 0:
            @pl.when(jnp.logical_and(place_in_plane == q, jnp.logical_not(last_plane)))
            def _(cross=cross):
                enter(cross)

    for name in ["ew2", "feat", "gain"] + [f"x{c}" for c in range(1, nc)]:
        loads[name].wait()
    for c in range(nc):
        for _ in range(1):
            wcol = jnp.concatenate([gwt[spot(c), b:b + 1] for b in range(nb)], axis=0)
            y = x[:, spot(c), :].reshape(m, depth).astype(F32) + dot(hid[c % 2], ew2[...])
            enc[:, spot(c), :] = y.astype(BF).reshape(nb, r, depth)
            wy = (y * wcol).astype(BF)
            if c < nc - 1:
                open_chunk(c + 1)
            part = dot(sel[...], wy)
        contribute(c, part)
        if c >= LAG:
            absorb(c - LAG)
    for q, cross, partner, target in EDGES:
        right = cross[0] < 0

        @pl.when(place_in_plane == q)
        def _(cross=cross, partner=partner, target=target, right=right, q=q):
            if right:
                open_right(nc, cross, partner, target)
            elif len(cross) == 1:
                cross_over(nc - 1, partner, target)
            for c in range(nc - LAG):
                presum(c, cross, q)

    for c in range(nc - LAG, nc - 1):
        absorb(c, True)

    loads["wqkv"].wait()
    loads["wout"].wait()
    for h in range(heads):
        cols = slice(2 * depth + h * HD, 2 * depth + (h + 1) * HD)
        wvo[h * depth:(h + 1) * depth, :] = dot(
            wqkv[:, cols], wout[h * HD:(h + 1) * HD, :]
        ).astype(BF)
    absorb(nc - 1, True)
    for q, cross, _, _ in EDGES:
        @pl.when(place_in_plane == q)
        def _(cross=cross):
            for c in range(nc):
                finish(c, (far(cross),), local(cross), r1x)

    parts = 2
    ar = rows // parts
    scale = HD ** -0.5
    q = dot(nall[OWN], wqkv[:, :depth]).astype(BF)
    for h in range(heads):
        t = scale * dot_nt(
            q[:, h * HD:(h + 1) * HD], wqkv[:, depth + h * HD:depth + (h + 1) * HD]
        )
        for p in range(parts):
            qt[p, h * ar:(h + 1) * ar, :] = t[p * ar:(p + 1) * ar].astype(BF)
    for p in range(parts):
        sown[p] = dot_nt(qt[p], nall[OWN])

    @pl.when(inner)
    def _():
        arrived(nall.at[0:OWN], r2.at[0])

    for q, cross, partner, target in EDGES:
        @pl.when(place_in_plane == q)
        def _(cross=cross, partner=partner, target=target, q=q):
            _, direct, onward, handed = SUMS[q]
            if direct:
                arrived(arecv.at[:, 0:len(direct)], r2x.at[0])
            if onward is not None:
                for c in range(nc):
                    passed(c, partner, onward).start()
            arrived(nall.at[0:OWN - len(cross)], r2.at[0])
            if handed is not None:
                arrived(arecv.at[:, 0:1], r2f.at[0])
            if len(cross) == 2:
                for c in range(nc):
                    arrived(xrecv.at[c], rx.at[c])
            for c in range(nc):
                for source in cross:
                    total = arecv[c, SLOT[-source]].astype(F32)
                    total = total + psend[c, SLOT[source]].astype(F32)
                    if source == target:
                        total = total + xrecv[c].astype(F32)
                    nall[SLOT[source], spot(c), :] = norm(total)

    per = nc // parts
    for p in range(parts):
        scores = dot_nt(qt[p], nall[0:OWN].reshape(OWN * rows, depth)) + bias[...]
        scores = jnp.concatenate([scores, sown[p]], axis=1)
        top = jnp.max(scores, axis=-1, keepdims=True)
        e = jnp.exp(scores - top)
        total = jnp.sum(e, axis=-1, keepdims=True)
        mixed = dot(e.astype(BF), nall[...].reshape(5 * rows, depth))
        mixed = (mixed / total).astype(BF)
        mixed = jnp.concatenate([mixed[h * ar:(h + 1) * ar] for h in range(heads)], axis=1)
        new = (state[p * ar:(p + 1) * ar, :] + dot(mixed, wvo[...])).astype(BF)
        mesh[p * ar:(p + 1) * ar, :] = new
        for i in range(per):
            c = p * per + i
            cands[c][2] = new[i * r:(i + 1) * r]
            for delta in DELTAS:
                third(c, delta).start()

    loads["dw1"].wait()
    loads["dw2"].wait()
    def read(c):
        arrived(psend.at[c], r3.at[c])
        pieces = []
        for b in range(nb):
            e = jnp.minimum(offset(mown[b]), 4)
            pieces.append(
                enc[b, spot(c), :].astype(F32)
                + mwt[spot(c), b:b + 1] * cands[c][e].astype(F32)
            )
        return jnp.concatenate(pieces, axis=0).astype(BF)

    rows_in = read(0)
    hidden_layer(rows_in, dw1, hid.at[0])
    for c in range(nc - 1):
        after = read(c + 1)
        for _ in range(1):
            y = rows_in.astype(F32) + dot(hid[c % 2], dw2[...])
            res[:, spot(c), :] = y.astype(BF).reshape(nb, r, depth)
            hidden_layer(after, dw1, hout if c == nc - 2 else hid.at[(c + 1) % 2])
        rows_in = after
    rin[...] = rows_in
    left(psend, ssem.at[3])

    @pl.when(inner)
    def _():
        for i in (0, 1):
            left(psend, ssem.at[i])

    for q, cross, _, _ in EDGES:
        @pl.when(place_in_plane == q)
        def _(cross=cross, q=q):
            for i in (0, 1):
                left(psend.at[:, 0:len(local(cross)) + 1], ssem.at[i])
            left(arecv.at[:, 0:1 if SUMS[q][2] is None else 2], ssem.at[2])


def last_kernel(res, rin, mesh, hid, dw2, dec_hbm, mesh_hbm, tail, sem):
    nb, rows, depth = res.shape
    m = rin.shape[0]
    r = m // nb
    done = rows - r
    outs = [
        pltpu.make_async_copy(
            res.at[:, 0:done, :], dec_hbm.at[:, 0:done, :], sem.at[0]
        ),
        pltpu.make_async_copy(mesh, mesh_hbm, sem.at[1]),
    ]
    for out in outs:
        out.start()
    y = rin[...].astype(F32) + dot(hid[...], dw2[...])
    tail[...] = y.astype(BF).reshape(nb, r, depth)
    out = pltpu.make_async_copy(tail, dec_hbm.at[:, done:, :], sem.at[2])
    out.start()
    outs.append(out)
    for out in outs:
        out.wait()


def on_device(
    grid, g2m_owner, g2m_weight, m2g_owner, m2g_weight, mesh_feat, neighbours,
    enc_w1, enc_w2, attn_gain, w_qkv, w_out, dec_w1, dec_w2,
):
    nb = g2m_owner.shape[0]
    rows, depth = mesh_feat.shape
    ff = enc_w1.shape[1]
    nc = CHUNKS
    r = rows // nc
    nd = len(DELTAS)
    heads = depth // HD
    any_spec = pl.BlockSpec(memory_space=pl.ANY)
    vm_spec = pl.BlockSpec(memory_space=pltpu.VMEM)
    dma = pltpu.SemaphoreType.DMA
    vm = pltpu.VMEM
    held = pl.pallas_call(
        step_kernel,
        out_shape=(
            vm((nb, rows, depth), BF),
            vm((nb * r, depth), BF),
            vm((rows, depth), BF),
            vm((nb * r, ff), BF),
            vm((ff, depth), BF),
        ),
        in_specs=[pl.BlockSpec(memory_space=pltpu.HBM)] * 14,
        out_specs=(vm_spec,) * 5,
        scratch_shapes=[
            vm((nb, rows, depth), BF),
            vm((nb, rows, depth), BF),
            vm((rows, depth), BF),
            vm((rows, depth), F32),
            vm((5, rows, depth), BF),
            vm((2, nb * r, ff), BF),
            vm((depth, ff), BF),
            vm((2, rows // 2 * heads, depth), BF),
            vm((2, rows // 2 * heads, rows), F32),
            vm((1, OWN * rows), F32),
            vm((heads * depth, depth), BF),
            vm((5 * r, nb * r), BF),
            vm((depth, ff), BF),
            vm((ff, depth), BF),
            vm((depth, 3 * depth), BF),
            vm((depth, depth), BF),
            vm((1, depth), F32),
            vm((nb, rows), F32),
            vm((nb, rows), F32),
            vm((rows, rows), F32),
            vm((rows, rows), F32),
            vm((nc, nd, r, depth), BF),
            vm((nc, nd, r, depth), BF),
            vm((nc, r, depth), BF),
            vm((nc, r, depth), BF),
            vm((nc, nd, r, depth), BF),
            vm((nc, r, depth), BF),
            pltpu.SMEM((nb,), jnp.int32),
            pltpu.SMEM((nb,), jnp.int32),
            pltpu.SMEM((1, 3), jnp.int32),
        ]
        + [vm((5, r, depth), BF)] * nc
        + [dma((22,))]
        + [dma((4,)), dma((nc,)), dma((nc,)), dma((1,)), dma((1,)), dma((1,)), dma((nc,)), dma((nc,))]
        + [pltpu.SemaphoreType.REGULAR],
        compiler_params=pltpu.CompilerParams(
            collective_id=0, has_side_effects=True, vmem_limit_bytes=40 * 2**20
        ),
        name="step",
    )(*[pltpu.with_memory_space_constraint(a, pltpu.HBM) for a in (
        grid.reshape(nb, rows, depth), g2m_owner, g2m_weight.reshape(nb, rows),
        m2g_owner, m2g_weight.reshape(nb, rows), mesh_feat, neighbours,
        enc_w1, enc_w2, attn_gain, w_qkv, w_out, dec_w1, dec_w2,
    )])
    decoded, mesh_out = pl.pallas_call(
        last_kernel,
        out_shape=(
            jax.ShapeDtypeStruct((nb, rows, depth), BF),
            jax.ShapeDtypeStruct((rows, depth), BF),
        ),
        in_specs=[vm_spec] * 5,
        out_specs=(any_spec, any_spec),
        scratch_shapes=[
            vm((nb, r, depth), BF),
            dma((3,)),
        ],
        compiler_params=pltpu.CompilerParams(vmem_limit_bytes=16 * 2**20),
        name="last",
    )(*[pltpu.with_memory_space_constraint(a, pltpu.VMEM) for a in held])
    return decoded.reshape(nb * rows, depth), mesh_out


def solution(mesh):
    cut = P(("tile", "sub"))
    cut2 = P(("tile", "sub"), None)
    in_specs = (cut2, cut, cut, cut, cut, cut2, cut2) + (P(),) * 7
    return jax.shard_map(
        on_device, mesh=mesh, in_specs=in_specs, out_specs=(cut2, cut2), check_vma=False
    )
```

```python
import functools

import jax
import jax.numpy as jnp
from jax import lax
from jax.experimental import pallas as pl
from jax.experimental.pallas import tpu as pltpu
from jax.sharding import PartitionSpec as P

HD = 128
DELTAS = (-2, 2, -1, 1)
SLOT = {-2: 0, -1: 1, 1: 2, 2: 3}
OWN = 4
CHUNKS = 4
LAG = 3
NEG = -1e30
PLANE = 32
SUMS = {
    0: (-1, (-2,), None, -1),
    1: (-2, (-2,), -2, None),
    PLANE - 2: (2, (), None, 2),
    PLANE - 1: (2, (1, 2), 1, None),
}
EDGES = (
    (0, (-2, -1), 1, -1),
    (1, (-2,), -1, -2),
    (PLANE - 2, (2,), 1, 2),
    (PLANE - 1, (1, 2), -1, 1),
)
BF = jnp.bfloat16
F32 = jnp.float32
NT = (((1,), (1,)), ((), ()))


def dot(a, b):
    return jnp.dot(a, b, preferred_element_type=F32)


def dot_nt(a, b):
    return lax.dot_general(a, b, NT, preferred_element_type=F32)


def crosses_up(position, delta):
    if delta < 0:
        return jnp.bool_(False)
    return jnp.logical_and(position < PLANE, position + delta >= PLANE)


def hidden_layer(rows, w1, hid):
    width = 512
    for f in range(0, w1.shape[1], width):
        cols = slice(f, f + width)
        half = 0.5 * dot(rows, w1[:, cols])
        hid[:, cols] = (half + half * jnp.tanh(half)).astype(BF)


def step_kernel(
    grid_hbm, gown_hbm, gw_hbm, mown_hbm, mw_hbm, feat_hbm, neigh_hbm,
    ew1_hbm, ew2_hbm, gain_hbm, wqkv_hbm, wout_hbm, dw1_hbm, dw2_hbm,
    res, rin, mesh, hout, dw2,
    x, enc, feat, state, nall, hid, dw1, qt, sown, bias, wvo, sel,
    ew1, ew2, wqkv, wout, gain, gw, mw, gwt, mwt,
    psend, precv, csend, asend, arecv, xrecv, gown, mown, neigh, *rest,
):
    nc = CHUNKS
    cands = rest[:nc]
    lsem, ssem, r1, r1x, r2, r2x, r2f, r3, rx, ready = rest[nc:]
    nb, rows, depth = x.shape
    heads = depth // HD
    r = rows // nc
    m = nb * r
    count = lax.axis_size("tile") * lax.axis_size("sub")
    me = lax.axis_index("tile") * lax.axis_size("sub") + lax.axis_index("sub")

    def place(delta):
        d = lax.rem(me + delta + count, count)
        return (d // 2, lax.rem(d, 2))

    def offset(block):
        return lax.rem(block - me + 2 + count, count)

    place_in_plane = lax.rem(me, PLANE)
    inner = jnp.logical_and(place_in_plane > 1, place_in_plane < PLANE - 2)
    last_plane = me >= count - PLANE

    def tell(sem, delta):
        pl.semaphore_signal(
            sem, inc=1, device_id=place(delta), device_id_type=pl.DeviceIdType.MESH
        )

    barrier = pltpu.get_barrier_semaphore()
    for delta in DELTAS:
        @pl.when(jnp.logical_not(crosses_up(place_in_plane, delta)))
        def _(delta=delta):
            tell(barrier, delta)

    def enter(cross):
        right = bool(cross) and cross[0] < 0
        pl.semaphore_wait(barrier, len(DELTAS) - (len(cross) if right else 0))
        if cross and not right:
            for delta in cross:
                tell(ready, delta)

    loads = {}

    def load(name, src, dst):
        c = pltpu.make_async_copy(src, dst, lsem.at[len(loads)])
        c.start()
        loads[name] = c

    load("gown", gown_hbm, gown)
    load("gw", gw_hbm, gw)
    load("mown", mown_hbm, mown)
    load("mw", mw_hbm, mw)
    load("neigh", neigh_hbm, neigh)
    load("gain", gain_hbm, gain)
    load("x0", grid_hbm.at[:, 0:r, :], x.at[:, 0:r, :])
    load("ew1", ew1_hbm, ew1)
    load("ew2", ew2_hbm, ew2)
    load("x1", grid_hbm.at[:, r:rows, :], x.at[:, r:rows, :])
    load("feat", feat_hbm, feat)

    for q, cross, _, _ in EDGES:
        if cross[0] > 0:
            @pl.when(jnp.logical_and(place_in_plane == q, last_plane))
            def _(cross=cross):
                enter(cross)

    for name in ("gown", "gw", "mown", "mw", "neigh"):
        loads[name].wait()
    gwt[...] = jnp.tile(gw[...], (rows // nb, 1)).T
    mwt[...] = jnp.tile(mw[...], (rows // nb, 1)).T

    out_row = lax.broadcasted_iota(jnp.int32, (r, r), 0)
    in_row = lax.broadcasted_iota(jnp.int32, (r, r), 1)
    same = (out_row == in_row).astype(F32)
    for b in range(nb):
        e = offset(gown[b])
        for s in range(5):
            hit = jnp.where(e == s, 1.0, 0.0).astype(F32)
            sel[s * r:(s + 1) * r, b * r:(b + 1) * r] = (same * hit).astype(BF)
    for delta, s in SLOT.items():
        listed = jnp.int32(0)
        for j in range(3):
            listed = listed + jnp.where(offset(neigh[0, j]) == 2 + delta, 1, 0)
        fill = jnp.where(listed > 0, 0.0, NEG).astype(F32)
        bias[:, s * rows:(s + 1) * rows] = jnp.full((1, rows), fill, F32)

    def remote(src, dst, ssem, rsem, delta):
        return pltpu.make_async_remote_copy(
            src_ref=src, dst_ref=dst, send_sem=ssem, recv_sem=rsem,
            device_id=place(delta), device_id_type=pl.DeviceIdType.MESH,
        )

    def spot(c):
        return slice(c * r, (c + 1) * r)

    def first(c, delta, cross=()):
        k = SLOT[delta]
        return remote(
            psend.at[c, k], precv.at[c, k], ssem.at[0],
            (r1x if delta in cross else r1).at[c], delta,
        )

    def second(c, delta):
        return remote(
            nall.at[OWN, spot(c), :], nall.at[SLOT[-delta], spot(c), :],
            ssem.at[1], r2.at[0], delta,
        )

    def across(c, delta):
        return remote(asend.at[c], arecv.at[c, SLOT[delta]], ssem.at[1], r2x.at[0], delta)

    def passed(c, partner, source):
        own, other = SLOT[-source], SLOT[partner - source]
        return remote(arecv.at[c, own], arecv.at[c, other], ssem.at[2], r2f.at[0], partner)

    def shared(c, partner, target):
        return remote(psend.at[c, SLOT[target]], xrecv.at[c], ssem.at[2], rx.at[c], partner)

    def both(c, target):
        k = SLOT[target]
        return remote(csend.at[c], precv.at[c, k], ssem.at[0], r1x.at[c], target)

    def cross_over(c, partner, target):
        if abs(target) == 2:
            arrived(xrecv.at[c], rx.at[c])
            csend[c] = (
                psend[c, SLOT[target]].astype(F32) + xrecv[c].astype(F32)
            ).astype(BF)
            both(c, target).start()
        else:
            first(c, 2 * target, (2 * target,)).start()

    def third(c, delta):
        cand = cands[c]
        return remote(cand.at[2], cand.at[2 - delta], ssem.at[3], r3.at[c], delta)

    def arrived(ref, sem):
        remote(ref, ref, ssem.at[0], sem, 1).wait_recv()

    def left(ref, sem):
        remote(ref, ref, sem, r1.at[0], 1).wait_send()

    def far(cross):
        return -2 if cross[0] < 0 else 2

    def local(cross):
        return [d for d in DELTAS if d not in cross]

    def norm(total):
        mean_sq = jnp.mean(total * total, axis=-1, keepdims=True)
        return (total * lax.rsqrt(mean_sq + 1e-06) * gain[...]).astype(BF)

    def add(c, sources):
        total = state[spot(c), :]
        for source in sources:
            total = total + precv[c, SLOT[-source]].astype(F32)
        state[spot(c), :] = total
        return total

    def finish(c, sources, targets, sem):
        arrived(precv.at[c, 0:len(sources)], sem.at[c])
        total = add(c, sources)
        nall[OWN, spot(c), :] = norm(total)
        for delta in targets:
            second(c, delta).start()

    def presum(c, cross, q):
        here = local(cross)
        arrived(precv.at[c, 0:len(here)], r1.at[c])
        asend[c] = add(c, here).astype(BF)
        across(c, SUMS[q][0]).start()

    def open_right(done, cross, partner, target):
        pl.semaphore_wait(ready, len(cross))
        for c in range(done):
            cross_over(c, partner, target)

    def absorb(c, late=False):
        @pl.when(inner)
        def _():
            finish(c, DELTAS, DELTAS, r1)

        if late:
            for q, cross, _, _ in EDGES:
                @pl.when(place_in_plane == q)
                def _(cross=cross, q=q):
                    presum(c, cross, q)

    def contribute(c, part):
        state[spot(c), :] = feat[spot(c), :].astype(F32) + part[2 * r:3 * r]
        for delta in DELTAS:
            psend[c, SLOT[delta]] = part[(2 + delta) * r:(3 + delta) * r].astype(BF)

        @pl.when(inner)
        def _():
            if c == 0:
                enter(())
            for delta in DELTAS:
                first(c, delta).start()

        for q, cross, partner, target in EDGES:
            right = cross[0] < 0

            @pl.when(place_in_plane == q)
            def _(cross=cross, partner=partner, target=target, right=right):
                if c == 0 and right:
                    enter(cross)
                for delta in local(cross):
                    first(c, delta, cross).start()
                shared(c, partner, target).start()
                if not right and len(cross) == 2:
                    cross_over(c, partner, target)
                if not right and len(cross) == 1 and c > 0:
                    cross_over(c - 1, partner, target)

    def open_chunk(c):
        hidden_layer(x[:, spot(c), :].reshape(m, depth), ew1, hid.at[c % 2])

    loads["x0"].wait()
    loads["ew1"].wait()
    load("wqkv", wqkv_hbm.at[0], wqkv)
    load("wout", wout_hbm.at[0], wout)
    load("dw1", dw1_hbm, dw1)
    load("dw2", dw2_hbm, dw2)
    open_chunk(0)
    for q, cross, _, _ in EDGES:
        if cross[0] > 0:
            @pl.when(jnp.logical_and(place_in_plane == q, jnp.logical_not(last_plane)))
            def _(cross=cross):
                enter(cross)

    for name in ("ew2", "feat", "gain", "x1"):
        loads[name].wait()
    for c in range(nc):
        for _ in range(1):
            wcol = jnp.concatenate([gwt[spot(c), b:b + 1] for b in range(nb)], axis=0)
            y = x[:, spot(c), :].reshape(m, depth).astype(F32) + dot(hid[c % 2], ew2[...])
            enc[:, spot(c), :] = y.astype(BF).reshape(nb, r, depth)
            wy = (y * wcol).astype(BF)
            if c < nc - 1:
                open_chunk(c + 1)
            part = dot(sel[...], wy)
        contribute(c, part)
        if c >= LAG:
            absorb(c - LAG)
    for q, cross, partner, target in EDGES:
        right = cross[0] < 0

        @pl.when(place_in_plane == q)
        def _(cross=cross, partner=partner, target=target, right=right, q=q):
            if right:
                open_right(nc, cross, partner, target)
            elif len(cross) == 1:
                cross_over(nc - 1, partner, target)
            for c in range(nc - LAG):
                presum(c, cross, q)

    for c in range(nc - LAG, nc - 1):
        absorb(c, True)

    loads["wqkv"].wait()
    loads["wout"].wait()
    for h in range(heads):
        cols = slice(2 * depth + h * HD, 2 * depth + (h + 1) * HD)
        wvo[h * depth:(h + 1) * depth, :] = dot(
            wqkv[:, cols], wout[h * HD:(h + 1) * HD, :]
        ).astype(BF)
    absorb(nc - 1, True)
    for q, cross, _, _ in EDGES:
        @pl.when(place_in_plane == q)
        def _(cross=cross):
            for c in range(nc):
                finish(c, (far(cross),), local(cross), r1x)

    parts = 2
    ar = rows // parts
    scale = HD ** -0.5
    q = dot(nall[OWN], wqkv[:, :depth]).astype(BF)
    for h in range(heads):
        t = scale * dot_nt(
            q[:, h * HD:(h + 1) * HD], wqkv[:, depth + h * HD:depth + (h + 1) * HD]
        )
        for p in range(parts):
            qt[p, h * ar:(h + 1) * ar, :] = t[p * ar:(p + 1) * ar].astype(BF)
    for p in range(parts):
        sown[p] = dot_nt(qt[p], nall[OWN])

    @pl.when(inner)
    def _():
        arrived(nall.at[0:OWN], r2.at[0])

    for q, cross, partner, target in EDGES:
        @pl.when(place_in_plane == q)
        def _(cross=cross, partner=partner, target=target, q=q):
            _, direct, onward, handed = SUMS[q]
            if direct:
                arrived(arecv.at[:, 0:len(direct)], r2x.at[0])
            if onward is not None:
                for c in range(nc):
                    passed(c, partner, onward).start()
            if len(cross) == 2:
                for c in range(nc):
                    arrived(xrecv.at[c], rx.at[c])

            def complete(source):
                for c in range(nc):
                    total = arecv[c, SLOT[-source]].astype(F32)
                    total = total + psend[c, SLOT[source]].astype(F32)
                    if source == target:
                        total = total + xrecv[c].astype(F32)
                    nall[SLOT[source], spot(c), :] = norm(total)

            for source in direct:
                complete(source)
            arrived(nall.at[0:OWN - len(cross)], r2.at[0])
            if handed is not None:
                arrived(arecv.at[:, 0:1], r2f.at[0])
                complete(handed)

    per = nc // parts
    for p in range(parts):
        scores = dot_nt(qt[p], nall[0:OWN].reshape(OWN * rows, depth)) + bias[...]
        scores = jnp.concatenate([scores, sown[p]], axis=1)
        top = jnp.max(scores, axis=-1, keepdims=True)
        e = jnp.exp(scores - top)
        total = jnp.sum(e, axis=-1, keepdims=True)
        mixed = dot(e.astype(BF), nall[...].reshape(5 * rows, depth))
        mixed = (mixed / total).astype(BF)
        mixed = jnp.concatenate([mixed[h * ar:(h + 1) * ar] for h in range(heads)], axis=1)
        new = (state[p * ar:(p + 1) * ar, :] + dot(mixed, wvo[...])).astype(BF)
        mesh[p * ar:(p + 1) * ar, :] = new
        for i in range(per):
            c = p * per + i
            cands[c][2] = new[i * r:(i + 1) * r]
            for delta in DELTAS:
                third(c, delta).start()

    loads["dw1"].wait()
    loads["dw2"].wait()
    def read(c):
        arrived(psend.at[c], r3.at[c])
        pieces = []
        for b in range(nb):
            e = jnp.minimum(offset(mown[b]), 4)
            pieces.append(
                enc[b, spot(c), :].astype(F32)
                + mwt[spot(c), b:b + 1] * cands[c][e].astype(F32)
            )
        return jnp.concatenate(pieces, axis=0).astype(BF)

    rows_in = read(0)
    hidden_layer(rows_in, dw1, hid.at[0])
    for c in range(nc - 1):
        after = read(c + 1)
        for _ in range(1):
            y = rows_in.astype(F32) + dot(hid[c % 2], dw2[...])
            res[:, spot(c), :] = y.astype(BF).reshape(nb, r, depth)
            hidden_layer(after, dw1, hout if c == nc - 2 else hid.at[(c + 1) % 2])
        rows_in = after
    rin[...] = rows_in
    left(psend, ssem.at[3])

    @pl.when(inner)
    def _():
        for i in (0, 1):
            left(psend, ssem.at[i])

    for q, cross, _, _ in EDGES:
        @pl.when(place_in_plane == q)
        def _(cross=cross, q=q):
            for i in (0, 1):
                left(psend.at[:, 0:len(local(cross)) + 1], ssem.at[i])
            left(arecv.at[:, 0:1 if SUMS[q][2] is None else 2], ssem.at[2])


def last_kernel(res, rin, mesh, hid, dw2, dec_hbm, mesh_hbm, tail, sem):
    nb, rows, depth = res.shape
    m = rin.shape[0]
    r = m // nb
    done = rows - r
    outs = [
        pltpu.make_async_copy(
            res.at[:, 0:done, :], dec_hbm.at[:, 0:done, :], sem.at[0]
        ),
        pltpu.make_async_copy(mesh, mesh_hbm, sem.at[1]),
    ]
    for out in outs:
        out.start()
    y = rin[...].astype(F32) + dot(hid[...], dw2[...])
    tail[...] = y.astype(BF).reshape(nb, r, depth)
    out = pltpu.make_async_copy(tail, dec_hbm.at[:, done:, :], sem.at[2])
    out.start()
    outs.append(out)
    for out in outs:
        out.wait()


def on_device(
    grid, g2m_owner, g2m_weight, m2g_owner, m2g_weight, mesh_feat, neighbours,
    enc_w1, enc_w2, attn_gain, w_qkv, w_out, dec_w1, dec_w2,
):
    nb = g2m_owner.shape[0]
    rows, depth = mesh_feat.shape
    ff = enc_w1.shape[1]
    nc = CHUNKS
    r = rows // nc
    nd = len(DELTAS)
    heads = depth // HD
    any_spec = pl.BlockSpec(memory_space=pl.ANY)
    vm_spec = pl.BlockSpec(memory_space=pltpu.VMEM)
    dma = pltpu.SemaphoreType.DMA
    vm = pltpu.VMEM
    held = pl.pallas_call(
        step_kernel,
        out_shape=(
            vm((nb, rows, depth), BF),
            vm((nb * r, depth), BF),
            vm((rows, depth), BF),
            vm((nb * r, ff), BF),
            vm((ff, depth), BF),
        ),
        in_specs=[pl.BlockSpec(memory_space=pltpu.HBM)] * 14,
        out_specs=(vm_spec,) * 5,
        scratch_shapes=[
            vm((nb, rows, depth), BF),
            vm((nb, rows, depth), BF),
            vm((rows, depth), BF),
            vm((rows, depth), F32),
            vm((5, rows, depth), BF),
            vm((2, nb * r, ff), BF),
            vm((depth, ff), BF),
            vm((2, rows // 2 * heads, depth), BF),
            vm((2, rows // 2 * heads, rows), F32),
            vm((1, OWN * rows), F32),
            vm((heads * depth, depth), BF),
            vm((5 * r, nb * r), BF),
            vm((depth, ff), BF),
            vm((ff, depth), BF),
            vm((depth, 3 * depth), BF),
            vm((depth, depth), BF),
            vm((1, depth), F32),
            vm((nb, rows), F32),
            vm((nb, rows), F32),
            vm((rows, rows), F32),
            vm((rows, rows), F32),
            vm((nc, nd, r, depth), BF),
            vm((nc, nd, r, depth), BF),
            vm((nc, r, depth), BF),
            vm((nc, r, depth), BF),
            vm((nc, nd, r, depth), BF),
            vm((nc, r, depth), BF),
            pltpu.SMEM((nb,), jnp.int32),
            pltpu.SMEM((nb,), jnp.int32),
            pltpu.SMEM((1, 3), jnp.int32),
        ]
        + [vm((5, r, depth), BF)] * nc
        + [dma((15,))]
        + [dma((4,)), dma((nc,)), dma((nc,)), dma((1,)), dma((1,)), dma((1,)), dma((nc,)), dma((nc,))]
        + [pltpu.SemaphoreType.REGULAR],
        compiler_params=pltpu.CompilerParams(
            collective_id=0, has_side_effects=True, vmem_limit_bytes=40 * 2**20
        ),
        name="step",
    )(*[pltpu.with_memory_space_constraint(a, pltpu.HBM) for a in (
        grid.reshape(nb, rows, depth), g2m_owner, g2m_weight.reshape(nb, rows),
        m2g_owner, m2g_weight.reshape(nb, rows), mesh_feat, neighbours,
        enc_w1, enc_w2, attn_gain, w_qkv, w_out, dec_w1, dec_w2,
    )])
    decoded, mesh_out = pl.pallas_call(
        last_kernel,
        out_shape=(
            jax.ShapeDtypeStruct((nb, rows, depth), BF),
            jax.ShapeDtypeStruct((rows, depth), BF),
        ),
        in_specs=[vm_spec] * 5,
        out_specs=(any_spec, any_spec),
        scratch_shapes=[
            vm((nb, r, depth), BF),
            dma((3,)),
        ],
        compiler_params=pltpu.CompilerParams(vmem_limit_bytes=16 * 2**20),
        name="last",
    )(*[pltpu.with_memory_space_constraint(a, pltpu.VMEM) for a in held])
    return decoded.reshape(nb * rows, depth), mesh_out


def solution(mesh):
    cut = P(("tile", "sub"))
    cut2 = P(("tile", "sub"), None)
    in_specs = (cut2, cut, cut, cut, cut, cut2, cut2) + (P(),) * 7
    return jax.shard_map(
        on_device, mesh=mesh, in_specs=in_specs, out_specs=(cut2, cut2), check_vma=False
    )
```

```python
import functools

import jax
import jax.numpy as jnp
from jax import lax
from jax.experimental import pallas as pl
from jax.experimental.pallas import tpu as pltpu
from jax.sharding import PartitionSpec as P

HD = 128
DELTAS = (-2, 2, -1, 1)
SLOT = {-2: 0, -1: 1, 1: 2, 2: 3}
OWN = 4
CHUNKS = 4
LAG = 3
NEG = -1e30
PLANE = 32
SUMS = {
    0: (-1, (-2,), None, -1),
    1: (-2, (-2,), -2, None),
    PLANE - 2: (2, (), None, 2),
    PLANE - 1: (2, (1, 2), 1, None),
}
EDGES = (
    (0, (-2, -1), 1, -1),
    (1, (-2,), -1, -2),
    (PLANE - 2, (2,), 1, 2),
    (PLANE - 1, (1, 2), -1, 1),
)
BF = jnp.bfloat16
F32 = jnp.float32
NT = (((1,), (1,)), ((), ()))


def dot(a, b):
    return jnp.dot(a, b, preferred_element_type=F32)


def dot_nt(a, b):
    return lax.dot_general(a, b, NT, preferred_element_type=F32)


def crosses_up(position, delta):
    if delta < 0:
        return jnp.bool_(False)
    return jnp.logical_and(position < PLANE, position + delta >= PLANE)


def hidden_layer(rows, w1, hid):
    width = 512
    for f in range(0, w1.shape[1], width):
        cols = slice(f, f + width)
        half = 0.5 * dot(rows, w1[:, cols])
        hid[:, cols] = (half + half * jnp.tanh(half)).astype(BF)


def step_kernel(
    grid_hbm, gown_hbm, gw_hbm, mown_hbm, mw_hbm, feat_hbm, neigh_hbm,
    ew1_hbm, ew2_hbm, gain_hbm, wqkv_hbm, wout_hbm, dw1_hbm, dw2_hbm,
    res, rin, mesh, hout, dw2,
    x, enc, feat, state, nall, hid, dw1, qt, sown, bias, wvo, sel,
    ew1, ew2, wqkv, wout, gain, gw, mw, gwt, mwt,
    psend, precv, csend, asend, arecv, xrecv, gown, mown, neigh, *rest,
):
    nc = CHUNKS
    cands = rest[:nc]
    lsem, ssem, r1, r1x, r2, r2x, r2f, r3, rx, ready = rest[nc:]
    nb, rows, depth = x.shape
    heads = depth // HD
    r = rows // nc
    m = nb * r
    count = lax.axis_size("tile") * lax.axis_size("sub")
    me = lax.axis_index("tile") * lax.axis_size("sub") + lax.axis_index("sub")

    def place(delta):
        d = lax.rem(me + delta + count, count)
        return (d // 2, lax.rem(d, 2))

    def offset(block):
        return lax.rem(block - me + 2 + count, count)

    place_in_plane = lax.rem(me, PLANE)
    inner = jnp.logical_and(place_in_plane > 1, place_in_plane < PLANE - 2)
    last_plane = me >= count - PLANE

    def tell(sem, delta):
        pl.semaphore_signal(
            sem, inc=1, device_id=place(delta), device_id_type=pl.DeviceIdType.MESH
        )

    barrier = pltpu.get_barrier_semaphore()
    for delta in DELTAS:
        @pl.when(jnp.logical_not(crosses_up(place_in_plane, delta)))
        def _(delta=delta):
            tell(barrier, delta)

    def enter(cross):
        right = bool(cross) and cross[0] < 0
        pl.semaphore_wait(barrier, len(DELTAS) - (len(cross) if right else 0))
        if cross and not right:
            for delta in cross:
                tell(ready, delta)

    loads = {}

    def load(name, src, dst):
        c = pltpu.make_async_copy(src, dst, lsem.at[len(loads)])
        c.start()
        loads[name] = c

    load("gown", gown_hbm, gown)
    load("gw", gw_hbm, gw)
    load("mown", mown_hbm, mown)
    load("mw", mw_hbm, mw)
    load("neigh", neigh_hbm, neigh)
    load("gain", gain_hbm, gain)
    load("x0", grid_hbm.at[:, 0:r, :], x.at[:, 0:r, :])
    load("ew1", ew1_hbm, ew1)
    load("ew2", ew2_hbm, ew2)
    load("x1", grid_hbm.at[:, r:rows, :], x.at[:, r:rows, :])
    load("feat", feat_hbm, feat)

    for q, cross, _, _ in EDGES:
        if cross[0] > 0:
            @pl.when(jnp.logical_and(place_in_plane == q, last_plane))
            def _(cross=cross):
                enter(cross)

    for name in ("gown", "gw", "mown", "mw", "neigh"):
        loads[name].wait()
    gwt[...] = jnp.tile(gw[...], (rows // nb, 1)).T
    mwt[...] = jnp.tile(mw[...], (rows // nb, 1)).T

    out_row = lax.broadcasted_iota(jnp.int32, (r, r), 0)
    in_row = lax.broadcasted_iota(jnp.int32, (r, r), 1)
    same = (out_row == in_row).astype(F32)
    for b in range(nb):
        e = offset(gown[b])
        for s in range(5):
            hit = jnp.where(e == s, 1.0, 0.0).astype(F32)
            sel[s * r:(s + 1) * r, b * r:(b + 1) * r] = (same * hit).astype(BF)
    for delta, s in SLOT.items():
        listed = jnp.int32(0)
        for j in range(3):
            listed = listed + jnp.where(offset(neigh[0, j]) == 2 + delta, 1, 0)
        fill = jnp.where(listed > 0, 0.0, NEG).astype(F32)
        bias[:, s * rows:(s + 1) * rows] = jnp.full((1, rows), fill, F32)

    def remote(src, dst, ssem, rsem, delta):
        return pltpu.make_async_remote_copy(
            src_ref=src, dst_ref=dst, send_sem=ssem, recv_sem=rsem,
            device_id=place(delta), device_id_type=pl.DeviceIdType.MESH,
        )

    def spot(c):
        return slice(c * r, (c + 1) * r)

    def first(c, delta, cross=()):
        k = SLOT[delta]
        return remote(
            psend.at[c, k], precv.at[c, k], ssem.at[0],
            (r1x if delta in cross else r1).at[c], delta,
        )

    def second(c, delta):
        return remote(
            nall.at[OWN, spot(c), :], nall.at[SLOT[-delta], spot(c), :],
            ssem.at[1], r2.at[0], delta,
        )

    def across(c, delta):
        return remote(asend.at[c], arecv.at[c, SLOT[delta]], ssem.at[1], r2x.at[0], delta)

    def passed(c, partner, source):
        own, other = SLOT[-source], SLOT[partner - source]
        return remote(arecv.at[c, own], arecv.at[c, other], ssem.at[2], r2f.at[0], partner)

    def shared(c, partner, target):
        return remote(psend.at[c, SLOT[target]], xrecv.at[c], ssem.at[2], rx.at[c], partner)

    def both(c, target):
        k = SLOT[target]
        return remote(csend.at[c], precv.at[c, k], ssem.at[0], r1x.at[c], target)

    def cross_over(c, partner, target):
        if abs(target) == 2:
            arrived(xrecv.at[c], rx.at[c])
            csend[c] = (
                psend[c, SLOT[target]].astype(F32) + xrecv[c].astype(F32)
            ).astype(BF)
            both(c, target).start()
        else:
            first(c, 2 * target, (2 * target,)).start()

    def third(c, delta):
        cand = cands[c]
        return remote(cand.at[2], cand.at[2 - delta], ssem.at[3], r3.at[c], delta)

    def arrived(ref, sem):
        remote(ref, ref, ssem.at[0], sem, 1).wait_recv()

    def left(ref, sem):
        remote(ref, ref, sem, r1.at[0], 1).wait_send()

    def far(cross):
        return -2 if cross[0] < 0 else 2

    def local(cross):
        return [d for d in DELTAS if d not in cross]

    def norm(total):
        mean_sq = jnp.mean(total * total, axis=-1, keepdims=True)
        return (total * lax.rsqrt(mean_sq + 1e-06) * gain[...]).astype(BF)

    def add(c, sources):
        total = state[spot(c), :]
        for source in sources:
            total = total + precv[c, SLOT[-source]].astype(F32)
        state[spot(c), :] = total
        return total

    def finish(c, sources, targets, sem):
        arrived(precv.at[c, 0:len(sources)], sem.at[c])
        total = add(c, sources)
        nall[OWN, spot(c), :] = norm(total)
        for delta in targets:
            second(c, delta).start()

    def presum(c, cross, q):
        here = local(cross)
        arrived(precv.at[c, 0:len(here)], r1.at[c])
        asend[c] = add(c, here).astype(BF)
        across(c, SUMS[q][0]).start()

    def open_right(done, cross, partner, target):
        pl.semaphore_wait(ready, len(cross))
        for c in range(done):
            cross_over(c, partner, target)

    def absorb(c, late=False):
        @pl.when(inner)
        def _():
            finish(c, DELTAS, DELTAS, r1)

        if late:
            for q, cross, _, _ in EDGES:
                @pl.when(place_in_plane == q)
                def _(cross=cross, q=q):
                    presum(c, cross, q)

    def contribute(c, part):
        state[spot(c), :] = feat[spot(c), :].astype(F32) + part[2 * r:3 * r]
        for delta in DELTAS:
            psend[c, SLOT[delta]] = part[(2 + delta) * r:(3 + delta) * r].astype(BF)

        @pl.when(inner)
        def _():
            if c == 0:
                enter(())
            for delta in DELTAS:
                first(c, delta).start()

        for q, cross, partner, target in EDGES:
            right = cross[0] < 0

            @pl.when(place_in_plane == q)
            def _(cross=cross, partner=partner, target=target, right=right):
                if c == 0 and right:
                    enter(cross)
                for delta in local(cross):
                    first(c, delta, cross).start()
                shared(c, partner, target).start()
                if not right and len(cross) == 2:
                    cross_over(c, partner, target)
                if not right and len(cross) == 1 and c > 0:
                    cross_over(c - 1, partner, target)

    def open_chunk(c):
        hidden_layer(x[:, spot(c), :].reshape(m, depth), ew1, hid.at[c % 2])

    loads["x0"].wait()
    loads["ew1"].wait()
    load("wqkv", wqkv_hbm.at[0], wqkv)
    load("wout", wout_hbm.at[0], wout)
    load("dw1", dw1_hbm, dw1)
    load("dw2", dw2_hbm, dw2)
    open_chunk(0)
    for q, cross, _, _ in EDGES:
        if cross[0] > 0:
            @pl.when(jnp.logical_and(place_in_plane == q, jnp.logical_not(last_plane)))
            def _(cross=cross):
                enter(cross)

    for name in ("ew2", "feat", "gain", "x1"):
        loads[name].wait()
    for c in range(nc):
        for _ in range(1):
            wcol = jnp.concatenate([gwt[spot(c), b:b + 1] for b in range(nb)], axis=0)
            y = x[:, spot(c), :].reshape(m, depth).astype(F32) + dot(hid[c % 2], ew2[...])
            enc[:, spot(c), :] = y.astype(BF).reshape(nb, r, depth)
            wy = (y * wcol).astype(BF)
            if c < nc - 1:
                open_chunk(c + 1)
            part = dot(sel[...], wy)
        contribute(c, part)
        if c >= LAG:
            absorb(c - LAG)
    for q, cross, partner, target in EDGES:
        right = cross[0] < 0

        @pl.when(place_in_plane == q)
        def _(cross=cross, partner=partner, target=target, right=right, q=q):
            if right:
                open_right(nc, cross, partner, target)
            elif len(cross) == 1:
                cross_over(nc - 1, partner, target)
            for c in range(nc - LAG):
                presum(c, cross, q)

    for c in range(nc - LAG, nc - 1):
        absorb(c, True)

    loads["wqkv"].wait()
    loads["wout"].wait()
    for h in range(heads):
        cols = slice(2 * depth + h * HD, 2 * depth + (h + 1) * HD)
        wvo[h * depth:(h + 1) * depth, :] = dot(
            wqkv[:, cols], wout[h * HD:(h + 1) * HD, :]
        ).astype(BF)
    absorb(nc - 1, True)
    for q, cross, _, _ in EDGES:
        @pl.when(place_in_plane == q)
        def _(cross=cross):
            for c in range(nc):
                finish(c, (far(cross),), local(cross), r1x)

    parts = 2
    ar = rows // parts
    scale = HD ** -0.5
    q = dot(nall[OWN], wqkv[:, :depth]).astype(BF)
    for h in range(heads):
        t = scale * dot_nt(
            q[:, h * HD:(h + 1) * HD], wqkv[:, depth + h * HD:depth + (h + 1) * HD]
        )
        for p in range(parts):
            qt[p, h * ar:(h + 1) * ar, :] = t[p * ar:(p + 1) * ar].astype(BF)
    for p in range(parts):
        sown[p] = dot_nt(qt[p], nall[OWN])

    @pl.when(inner)
    def _():
        arrived(nall.at[0:OWN], r2.at[0])

    for q, cross, partner, target in EDGES:
        @pl.when(place_in_plane == q)
        def _(cross=cross, partner=partner, target=target, q=q):
            _, direct, onward, handed = SUMS[q]
            if direct:
                arrived(arecv.at[:, 0:len(direct)], r2x.at[0])
            if onward is not None:
                for c in range(nc):
                    passed(c, partner, onward).start()
            if len(cross) == 2:
                for c in range(nc):
                    arrived(xrecv.at[c], rx.at[c])

            def complete(source):
                for c in range(nc):
                    total = arecv[c, SLOT[-source]].astype(F32)
                    total = total + psend[c, SLOT[source]].astype(F32)
                    if source == target:
                        total = total + xrecv[c].astype(F32)
                    nall[SLOT[source], spot(c), :] = norm(total)

            for source in direct:
                complete(source)
            arrived(nall.at[0:OWN - len(cross)], r2.at[0])
            if handed is not None:
                arrived(arecv.at[:, 0:1], r2f.at[0])
                complete(handed)

    per = nc // parts
    for p in range(parts):
        scores = dot_nt(qt[p], nall[0:OWN].reshape(OWN * rows, depth)) + bias[...]
        scores = jnp.concatenate([scores, sown[p]], axis=1)
        top = jnp.max(scores, axis=-1, keepdims=True)
        e = jnp.exp(scores - top)
        total = jnp.sum(e, axis=-1, keepdims=True)
        mixed = dot(e.astype(BF), nall[...].reshape(5 * rows, depth))
        mixed = (mixed / total).astype(BF)
        mixed = jnp.concatenate([mixed[h * ar:(h + 1) * ar] for h in range(heads)], axis=1)
        new = (state[p * ar:(p + 1) * ar, :] + dot(mixed, wvo[...])).astype(BF)
        mesh[p * ar:(p + 1) * ar, :] = new
        for i in range(per):
            c = p * per + i
            cands[c][2] = new[i * r:(i + 1) * r]
            for delta in DELTAS:
                third(c, delta).start()

    loads["dw1"].wait()
    loads["dw2"].wait()
    def read(c):
        arrived(psend.at[c], r3.at[c])
        pieces = []
        for b in range(nb):
            e = jnp.minimum(offset(mown[b]), 4)
            pieces.append(
                enc[b, spot(c), :].astype(F32)
                + mwt[spot(c), b:b + 1] * cands[c][e].astype(F32)
            )
        return jnp.concatenate(pieces, axis=0).astype(BF)

    rows_in = read(0)
    hidden_layer(rows_in, dw1, hid.at[0])
    for c in range(nc - 1):
        after = read(c + 1)
        for _ in range(1):
            y = rows_in.astype(F32) + dot(hid[c % 2], dw2[...])
            res[:, spot(c), :] = y.astype(BF).reshape(nb, r, depth)
            hidden_layer(after, dw1, hout if c == nc - 2 else hid.at[(c + 1) % 2])
        rows_in = after
    rin[...] = rows_in
    left(psend, ssem.at[3])

    @pl.when(inner)
    def _():
        for i in (0, 1):
            left(psend, ssem.at[i])

    for q, cross, _, _ in EDGES:
        @pl.when(place_in_plane == q)
        def _(cross=cross, q=q):
            for i in (0, 1):
                left(psend.at[:, 0:len(local(cross)) + 1], ssem.at[i])
            left(arecv.at[:, 0:1 if SUMS[q][2] is None else 2], ssem.at[2])


def last_kernel(res, rin, mesh, hid, dw2, dec_hbm, mesh_hbm, tail, sem):
    nb, rows, depth = res.shape
    m = rin.shape[0]
    r = m // nb
    done = rows - r
    outs = [
        pltpu.make_async_copy(
            res.at[:, 0:done, :], dec_hbm.at[:, 0:done, :], sem.at[0]
        ),
        pltpu.make_async_copy(mesh, mesh_hbm, sem.at[1]),
    ]
    for out in outs:
        out.start()
    half = dw2.shape[1] // 2
    for i in range(2):
        cols = slice(i * half, (i + 1) * half)
        y = rin[:, cols].astype(F32) + dot(hid[...], dw2[:, cols])
        tail[:, :, cols] = y.astype(BF).reshape(nb, r, half)
        out = pltpu.make_async_copy(
            tail.at[:, :, cols], dec_hbm.at[:, done:, cols], sem.at[2 + i]
        )
        out.start()
        outs.append(out)
    for out in outs:
        out.wait()


def on_device(
    grid, g2m_owner, g2m_weight, m2g_owner, m2g_weight, mesh_feat, neighbours,
    enc_w1, enc_w2, attn_gain, w_qkv, w_out, dec_w1, dec_w2,
):
    nb = g2m_owner.shape[0]
    rows, depth = mesh_feat.shape
    ff = enc_w1.shape[1]
    nc = CHUNKS
    r = rows // nc
    nd = len(DELTAS)
    heads = depth // HD
    any_spec = pl.BlockSpec(memory_space=pl.ANY)
    vm_spec = pl.BlockSpec(memory_space=pltpu.VMEM)
    dma = pltpu.SemaphoreType.DMA
    vm = pltpu.VMEM
    held = pl.pallas_call(
        step_kernel,
        out_shape=(
            vm((nb, rows, depth), BF),
            vm((nb * r, depth), BF),
            vm((rows, depth), BF),
            vm((nb * r, ff), BF),
            vm((ff, depth), BF),
        ),
        in_specs=[pl.BlockSpec(memory_space=pltpu.HBM)] * 14,
        out_specs=(vm_spec,) * 5,
        scratch_shapes=[
            vm((nb, rows, depth), BF),
            vm((nb, rows, depth), BF),
            vm((rows, depth), BF),
            vm((rows, depth), F32),
            vm((5, rows, depth), BF),
            vm((2, nb * r, ff), BF),
            vm((depth, ff), BF),
            vm((2, rows // 2 * heads, depth), BF),
            vm((2, rows // 2 * heads, rows), F32),
            vm((1, OWN * rows), F32),
            vm((heads * depth, depth), BF),
            vm((5 * r, nb * r), BF),
            vm((depth, ff), BF),
            vm((ff, depth), BF),
            vm((depth, 3 * depth), BF),
            vm((depth, depth), BF),
            vm((1, depth), F32),
            vm((nb, rows), F32),
            vm((nb, rows), F32),
            vm((rows, rows), F32),
            vm((rows, rows), F32),
            vm((nc, nd, r, depth), BF),
            vm((nc, nd, r, depth), BF),
            vm((nc, r, depth), BF),
            vm((nc, r, depth), BF),
            vm((nc, nd, r, depth), BF),
            vm((nc, r, depth), BF),
            pltpu.SMEM((nb,), jnp.int32),
            pltpu.SMEM((nb,), jnp.int32),
            pltpu.SMEM((1, 3), jnp.int32),
        ]
        + [vm((5, r, depth), BF)] * nc
        + [dma((15,))]
        + [dma((4,)), dma((nc,)), dma((nc,)), dma((1,)), dma((1,)), dma((1,)), dma((nc,)), dma((nc,))]
        + [pltpu.SemaphoreType.REGULAR],
        compiler_params=pltpu.CompilerParams(
            collective_id=0, has_side_effects=True, vmem_limit_bytes=40 * 2**20
        ),
        name="step",
    )(*[pltpu.with_memory_space_constraint(a, pltpu.HBM) for a in (
        grid.reshape(nb, rows, depth), g2m_owner, g2m_weight.reshape(nb, rows),
        m2g_owner, m2g_weight.reshape(nb, rows), mesh_feat, neighbours,
        enc_w1, enc_w2, attn_gain, w_qkv, w_out, dec_w1, dec_w2,
    )])
    decoded, mesh_out = pl.pallas_call(
        last_kernel,
        out_shape=(
            jax.ShapeDtypeStruct((nb, rows, depth), BF),
            jax.ShapeDtypeStruct((rows, depth), BF),
        ),
        in_specs=[vm_spec] * 5,
        out_specs=(any_spec, any_spec),
        scratch_shapes=[
            vm((nb, r, depth), BF),
            dma((4,)),
        ],
        compiler_params=pltpu.CompilerParams(vmem_limit_bytes=16 * 2**20),
        name="last",
    )(*[pltpu.with_memory_space_constraint(a, pltpu.VMEM) for a in held])
    return decoded.reshape(nb * rows, depth), mesh_out


def solution(mesh):
    cut = P(("tile", "sub"))
    cut2 = P(("tile", "sub"), None)
    in_specs = (cut2, cut, cut, cut, cut, cut2, cut2) + (P(),) * 7
    return jax.shard_map(
        on_device, mesh=mesh, in_specs=in_specs, out_specs=(cut2, cut2), check_vma=False
    )
```
